128 devices in a mesh: row: 8 (over y, x_hi), col: 16 (over z, x_lo, core).
Axes of the slice: x: 4 (x_hi: 2, x_lo: 2; x = x_hi * 2 + x_lo), y: 4, z: 4, core: 2. Of those that a mesh axis runs over, the one named last changes fastest.
Arguments:
- object_tiles: float32 [2, 2, 2048, 4096], P(None, None, 'row', 'col'), may hold values from -5 to 5
- probe_modes: float32 [2, 4, 128, 128], replicated, may hold values from -6 to 6
- offsets: int32 [8, 16, 3, 2], P('row', 'col'), may hold values from 0 to 192
- amplitude: float32 [8, 16, 3, 128, 128], P('row', 'col'), may hold values from 0.2 to 3
Outputs:
- object_grad: float32 [2, 2, 2048, 4096], P(None, None, 'row', 'col')
- probe_new: float32 [2, 4, 128, 128], replicated
The draws below stay inside these ranges and needn't reach their ends.
All inputs are finite; a program needn't handle non-finite values.
Results may differ from the reference program's by a relative error of at most 0.0003.
Values sent between devices are 32-bit elements; how exact they have to be, the bound alone decides.
No kernel may reach another device: no remote copies, remote signals or barrier semaphores. Data moves between devices by JAX's collectives and lax.ppermute only.
A program may use at most 64 MiB of HBM per device.

```python
import jax
import jax.numpy as jnp
from jax import lax

TILE = 256
HALO = 32
WIN = 128
MODES = 4
SLICES = 2
SCANS = 3
OBJ_ROWS = 2048
OBJ_COLS = 4096
N_ROW = 8
N_COL = 16


def plant(entries, key, least, top_value):
    shape = entries.shape
    index_at = [jax.random.randint(jax.random.fold_in(key, axis), (), 0, shape[axis]) for axis in range(len(shape))]
    entries = entries.at[tuple(index_at)].set(least)
    longest = shape.index(max(shape))
    index_at[longest] = (index_at[longest] + 1) % shape[longest]
    return entries.at[tuple(index_at)].set(top_value)


def block_scale(stream_key, dims, shards, low, top_value):
    def one(position, shards_of):
        heights = jax.random.uniform(jax.random.fold_in(jax.random.fold_in(stream_key, 6), position), (shards_of,), jnp.float32, low / len(shards), top_value / len(shards))
        return jnp.repeat(jnp.exp(heights), dims[position] // shards_of).reshape((-1,) + (1,) * (len(dims) - position - 1))

    gain = one(*shards[0])
    for cut in shards[1:]:
        gain = gain * one(*cut)
    return gain


def centred(own_key, extent, spread, limit, cuts=(), held_as=jnp.bfloat16):
    drawn = spread * jax.random.normal(own_key, extent, jnp.float32)
    if cuts:
        drawn = drawn * block_scale(own_key, extent, cuts, -0.22, 0.18)
    return jnp.clip(drawn, -limit, limit).astype(held_as)


def setup_inputs(seed: int = 0) -> dict:
    splits = jax.random.split(jax.random.key(seed), 5)
    return {
        "object_tiles": centred(splits[0], (2, SLICES, OBJ_ROWS, OBJ_COLS), 0.7, 5.0, ((2, 8), (3, 16)), jnp.float32),
        "probe_modes": centred(splits[1], (2, MODES, WIN, WIN), 1.0, 6.0, (), jnp.float32),
        "offsets": plant(jax.random.randint(splits[2], (N_ROW, N_COL, SCANS, 2), 0, TILE + 2 * HALO - WIN + 1), jax.random.fold_in(splits[2], 1), 0, TILE + 2 * HALO - WIN).astype(jnp.int32),
        "amplitude": jnp.clip(0.2 + 2.8 * jax.random.uniform(splits[3], (N_ROW, N_COL, SCANS, WIN, WIN), jnp.float32) ** block_scale(splits[3], (N_ROW, N_COL, SCANS, WIN, WIN), ((0, 8), (1, 16)), -0.2, 0.2), 0.2, 3.0),
    }


PROP = 0.002
SHIFT_AMP = 0.5
STEP_SIZE = 0.5
EPSILON = 1e-06
HIGH = lax.Precision.HIGHEST

def tables():
    counter = jnp.arange(WIN, dtype=jnp.int32)
    product = counter[:, None] * counter[None, :] % WIN
    angles = product.astype(jnp.float32) * (2.0 * jnp.pi / WIN)
    scale_factor = 1.0 / jnp.sqrt(jnp.float32(WIN))
    cos_table = jnp.cos(angles) * scale_factor
    sin_table = jnp.sin(angles) * scale_factor
    frequency = ((counter + WIN // 2) % WIN - WIN // 2).astype(jnp.float32)
    phase_map = -PROP * (frequency[:, None] ** 2 + frequency[None, :] ** 2)
    return (cos_table, sin_table, jnp.cos(phase_map), jnp.sin(phase_map))

def matprod(left_op, right_op):
    return jnp.matmul(left_op, right_op, precision=HIGH)

def transform(wave_real, wave_imag, sign_value, cos_table, sin_table):
    first_real = matprod(cos_table, wave_real) + sign_value * matprod(sin_table, wave_imag)
    first_imag = matprod(cos_table, wave_imag) - sign_value * matprod(sin_table, wave_real)
    second_real = matprod(first_real, cos_table) + sign_value * matprod(first_imag, sin_table)
    second_imag = matprod(first_imag, cos_table) - sign_value * matprod(first_real, sin_table)
    return (second_real, second_imag)

def position_loss(window, probe_field, measured, table_set):
    cos_table, sin_table, prop_cos, prop_sin = table_set
    probe_real = probe_field[0]
    probe_imag = probe_field[1]
    wave_real = probe_real * window[0, 0] - probe_imag * window[1, 0]
    wave_imag = probe_real * window[1, 0] + probe_imag * window[0, 0]
    for layer_no in range(1, SLICES):
        wave_real, wave_imag = transform(wave_real, wave_imag, 1.0, cos_table, sin_table)
        turned_real = wave_real * prop_cos - wave_imag * prop_sin
        turned_imag = wave_real * prop_sin + wave_imag * prop_cos
        wave_real, wave_imag = transform(turned_real, turned_imag, -1.0, cos_table, sin_table)
        slice_real = window[0, layer_no]
        slice_imag = window[1, layer_no]
        wave_real, wave_imag = (wave_real * slice_real - wave_imag * slice_imag, wave_real * slice_imag + wave_imag * slice_real)
    far_real, far_imag = transform(wave_real, wave_imag, 1.0, cos_table, sin_table)
    intensity = lax.optimization_barrier(jnp.sum(far_real * far_real + far_imag * far_imag, axis=0))
    return jnp.sum((jnp.sqrt(intensity + SHIFT_AMP) - measured) ** 2)

def update_probe(probe_field, gradient):
    mean_square = jnp.sum(gradient * gradient) / (2 * MODES * WIN * WIN)
    return probe_field - STEP_SIZE * gradient / jnp.sqrt(mean_square + EPSILON)

def reference(object_tiles, probe_modes, offsets, amplitude):
    table_set = tables()
    obj_rows = object_tiles.shape[2]
    obj_cols = object_tiles.shape[3]
    flat_offsets = offsets.reshape(-1, 2)
    flat_amp = amplitude.reshape(-1, WIN, WIN)
    numbers = jnp.arange(flat_offsets.shape[0], dtype=jnp.int32)
    window_span = jnp.arange(WIN, dtype=jnp.int32)

    def total_loss(tiles_field, probe_field):

        def step_fn(loss_acc, scan_item):
            number, shift_pair, measured = scan_item
            grid_row = number // (N_COL * SCANS)
            grid_col = number // SCANS % N_COL
            row_start = grid_row * TILE - HALO + shift_pair[0]
            col_start = grid_col * TILE - HALO + shift_pair[1]
            row_index = ((row_start + window_span) % obj_rows).astype(jnp.int32)
            col_index = ((col_start + window_span) % obj_cols).astype(jnp.int32)
            window = jnp.take(jnp.take(tiles_field, row_index, axis=2), col_index, axis=3)
            return (loss_acc + position_loss(window, probe_field, measured, table_set), None)
        loss_sum, _ = lax.scan(step_fn, jnp.zeros((), jnp.float32), (numbers, flat_offsets, flat_amp))
        return loss_sum
    grad_tiles, grad_probe = jax.grad(total_loss, argnums=(0, 1))(object_tiles, probe_modes)
    return (grad_tiles, update_probe(probe_modes, grad_probe))
```

```python
import functools

import jax
import jax.numpy as jnp
import numpy as np
from jax import lax
from jax.experimental import pallas as pl
from jax.experimental.pallas import tpu as pltpu
from jax.sharding import PartitionSpec as P

HALO = 32
WIN = 128
MODES = 4
PLANES = 4
LANES = 128
PROP = 0.002
SHIFT_AMP = 0.5
STEP_SIZE = 0.5
EPSILON = 1e-06
BOTH = ("row", "col")


def matrices():
    k = np.arange(WIN)
    c = np.exp(-2j * np.pi * (np.outer(k, k) % WIN) / WIN) / np.sqrt(WIN)
    f = ((k + WIN // 2) % WIN - WIN // 2).astype(np.float64)
    g = c.conj() @ np.diag(np.exp(-1j * PROP * f * f)) @ c
    stack = []
    for m in (c, c.conj(), g, g.conj()):
        w = np.block([[m.real, m.imag], [-m.imag, m.real]]).astype(np.float32)
        high = w.astype(jnp.bfloat16)
        low = (w - high.astype(np.float32)).astype(jnp.bfloat16)
        stack.append(np.stack([high, low]))
    return np.stack(stack)


C, C_CONJ, G, G_CONJ = range(4)


def lane_iota(rows):
    return lax.broadcasted_iota(jnp.int32, (rows, LANES), 1)


def pack_kernel(tile_ref, north_ref, south_ref, east_ref, west_ref):
    def strip(src, lo, rows):
        lane = lane_iota(rows)
        east = jnp.zeros((rows, LANES), jnp.float32)
        west = jnp.zeros((rows, LANES), jnp.float32)
        for p in range(PLANES):
            here = (lane >= p * HALO) & (lane < (p + 1) * HALO)
            right = src[p, :, LANES : 2 * LANES]
            left = src[p, :, 0:LANES]
            shift = (p * HALO - 3 * HALO) % LANES
            right = pltpu.roll(right, shift, 1) if shift else right
            left = pltpu.roll(left, p * HALO, 1) if p else left
            east = jnp.where(here, right, east)
            west = jnp.where(here, left, west)
        east_ref[lo : lo + rows, :] = east
        west_ref[lo : lo + rows, :] = west

    strip(north_ref, 0, HALO)
    strip(tile_ref, HALO, tile_ref.shape[1])
    strip(south_ref, HALO + tile_ref.shape[1], HALO)


def split(value):
    high = value.astype(jnp.bfloat16)
    return high, (value - high.astype(jnp.float32)).astype(jnp.bfloat16)


def dot(left, right):
    return jnp.dot(left, right, preferred_element_type=jnp.float32)


def main_kernel(
    offsets_ref, tile_ref, north_ref, south_ref, from_west_ref, from_east_ref, probe_ref, amp_ref, mat_ref,
    probe_grad_ref, core_grad_ref, east_rim_ref, west_rim_ref,
    ext, grad, rh, rl, lh, ll, field, d_keep,
):
    rows = tile_ref.shape[1]
    ext_rows = rows + 2 * HALO
    lane_all = lane_iota(ext_rows)
    for p in range(PLANES):
        for q in range(2):
            cols = slice(q * LANES, (q + 1) * LANES)
            ext[p, q, 0:HALO, :] = north_ref[p, :, cols]
            ext[p, q, HALO : HALO + rows, :] = tile_ref[p, :, cols]
            ext[p, q, HALO + rows : ext_rows, :] = south_ref[p, :, cols]
        right = from_east_ref[...]
        left = from_west_ref[...]
        right = pltpu.roll(right, (-p * HALO) % LANES, 1) if p else right
        shift = (3 * HALO - p * HALO) % LANES
        left = pltpu.roll(left, shift, 1) if shift else left
        ext[p, 2, :, :] = jnp.where(lane_all < 2 * HALO, right, left)
        ext[p, 3, :, :] = ext[p, 0, :, :]
    grad[...] = jnp.zeros_like(grad)
    probe_grad_ref[...] = jnp.zeros_like(probe_grad_ref)

    lane = lane_iota(WIN)
    half = WIN

    def put_r(m, real, imag):
        h, l = split(real)
        rh[m * WIN : (m + 1) * WIN, 0:half] = h
        rl[m * WIN : (m + 1) * WIN, 0:half] = l
        h, l = split(imag)
        rh[m * WIN : (m + 1) * WIN, half:] = h
        rl[m * WIN : (m + 1) * WIN, half:] = l

    def put_l(m, real, imag):
        h, l = split(real)
        lh[0:half, m * WIN : (m + 1) * WIN] = h
        ll[0:half, m * WIN : (m + 1) * WIN] = l
        h, l = split(imag)
        lh[half:, m * WIN : (m + 1) * WIN] = h
        ll[half:, m * WIN : (m + 1) * WIN] = l

    def from_right(which):
        high, low = mat_ref[which, 0], mat_ref[which, 1]
        out = dot(rh[...], high) + dot(rl[...], high) + dot(rh[...], low)
        return [
            (out[m * WIN : (m + 1) * WIN, 0:half], out[m * WIN : (m + 1) * WIN, half:]) for m in range(MODES)
        ]

    def from_left(which):
        high, low = mat_ref[which ^ 1, 0], mat_ref[which ^ 1, 1]
        out = dot(high, lh[...]) + dot(high, ll[...]) + dot(low, lh[...])
        return [
            (out[0:half, m * WIN : (m + 1) * WIN], out[half:, m * WIN : (m + 1) * WIN]) for m in range(MODES)
        ]

    def scan_step(s, carry):
        row = offsets_ref[2 * s]
        start = lax.rem(offsets_ref[2 * s + 1] + (3 * LANES - HALO), 3 * LANES)
        q = lax.div(start, LANES)
        shift = lax.rem(start, LANES)
        back = lax.rem(LANES - shift, LANES)

        def window(p):
            a = pltpu.roll(ext[p, q, pl.ds(row, WIN), :], back, 1)
            b = pltpu.roll(ext[p, q + 1, pl.ds(row, WIN), :], back, 1)
            return jnp.where(lane < LANES - shift, a, b)

        def scatter(p, value):
            moved = pltpu.roll(value, shift, 1)
            grad[p, q, pl.ds(row, WIN), :] += jnp.where(lane >= shift, moved, 0.0)
            q2 = lax.rem(q + 1, 3)
            grad[p, q2, pl.ds(row, WIN), :] += jnp.where(lane < shift, moved, 0.0)

        first_r, second_r, first_i, second_i = (window(p) for p in range(PLANES))
        for m in range(MODES):
            pr, pi = probe_ref[0, m], probe_ref[1, m]
            put_r(m, pr * first_r - pi * first_i, pr * first_i + pi * first_r)
        for m, (real, imag) in enumerate(from_right(G)):
            put_l(m, real, imag)
        for m, (real, imag) in enumerate(from_left(G)):
            d_keep[0, m] = real
            d_keep[1, m] = imag
            put_l(m, real * second_r - imag * second_i, real * second_i + imag * second_r)
        for m, (real, imag) in enumerate(from_left(C)):
            put_r(m, real, imag)
        intensity = jnp.full((WIN, WIN), SHIFT_AMP, jnp.float32)
        for m, (real, imag) in enumerate(from_right(C)):
            field[0, m] = real
            field[1, m] = imag
            intensity = intensity + (real * real + imag * imag)
        factor = 2.0 - 2.0 * amp_ref[s] / jnp.sqrt(intensity)
        for m in range(MODES):
            put_r(m, field[0, m] * factor, field[1, m] * factor)
        for m, (real, imag) in enumerate(from_right(C_CONJ)):
            put_l(m, real, imag)
        sum_r = jnp.zeros((WIN, WIN), jnp.float32)
        sum_i = jnp.zeros((WIN, WIN), jnp.float32)
        for m, (real, imag) in enumerate(from_left(C_CONJ)):
            dr, di = d_keep[0, m], d_keep[1, m]
            sum_r = sum_r + (dr * real + di * imag)
            sum_i = sum_i + (dr * imag - di * real)
            put_l(m, second_r * real + second_i * imag, second_r * imag - second_i * real)
        scatter(1, sum_r)
        scatter(3, sum_i)
        for m, (real, imag) in enumerate(from_left(G_CONJ)):
            put_r(m, real, imag)
        sum_r = jnp.zeros((WIN, WIN), jnp.float32)
        sum_i = jnp.zeros((WIN, WIN), jnp.float32)
        for m, (real, imag) in enumerate(from_right(G_CONJ)):
            pr, pi = probe_ref[0, m], probe_ref[1, m]
            sum_r = sum_r + (pr * real + pi * imag)
            sum_i = sum_i + (pr * imag - pi * real)
            probe_grad_ref[0, m] += first_r * real + first_i * imag
            probe_grad_ref[1, m] += first_r * imag - first_i * real
        scatter(0, sum_r)
        scatter(2, sum_i)
        return carry

    lax.fori_loop(0, amp_ref.shape[0], scan_step, 0)

    east = jnp.zeros((ext_rows, LANES), jnp.float32)
    west = jnp.zeros((ext_rows, LANES), jnp.float32)
    for p in range(PLANES):
        core_grad_ref[p] = grad[p, 0:2]
        third = grad[p, 2]
        here = (lane_all >= p * HALO) & (lane_all < (p + 1) * HALO)
        shift = (p * HALO - 3 * HALO) % LANES
        east = jnp.where(here, pltpu.roll(third, p * HALO, 1) if p else third, east)
        west = jnp.where(here, pltpu.roll(third, shift, 1) if shift else third, west)
    east_rim_ref[...] = east
    west_rim_ref[...] = west


def middle_kernel(
    core_ref, from_west_ref, from_east_ref, parts_ref, north_ref, south_ref, center_ref, share_ref
):
    share = jnp.sum(parts_ref[...], axis=0)
    share_ref[...] = jnp.broadcast_to(share[None], share_ref.shape)
    ext_rows = core_ref.shape[2]
    rows = ext_rows - 2 * HALO
    lane = lane_iota(ext_rows)
    for p in range(PLANES):
        left = from_west_ref[...]
        right = from_east_ref[...]
        left = pltpu.roll(left, (-p * HALO) % LANES, 1) if p else left
        shift = (3 * HALO - p * HALO) % LANES
        right = pltpu.roll(right, shift, 1) if shift else right
        cols = (
            core_ref[p, 0] + jnp.where(lane < HALO, left, 0.0),
            core_ref[p, 1] + jnp.where(lane >= LANES - HALO, right, 0.0),
        )
        for q in range(2):
            at = slice(q * LANES, (q + 1) * LANES)
            north_ref[p, :, at] = cols[q][0:HALO]
            center_ref[p, :, at] = cols[q][HALO : HALO + rows]
            south_ref[p, :, at] = cols[q][HALO + rows :]


def final_kernel(center_ref, from_north_ref, from_south_ref, total_ref, probe_ref, object_ref, probe_new_ref):
    rows = center_ref.shape[1]
    object_ref[:, HALO : rows - HALO, :] = center_ref[:, HALO : rows - HALO, :]
    object_ref[:, 0:HALO, :] = center_ref[:, 0:HALO, :] + from_north_ref[...]
    object_ref[:, rows - HALO :, :] = center_ref[:, rows - HALO :, :] + from_south_ref[...]
    total = total_ref[...]
    squares = jnp.sum(total * total, axis=0, keepdims=True)
    mean = jnp.sum(squares, axis=1, keepdims=True) / (total.shape[0] * total.shape[1])
    probe_new_ref[...] = probe_ref[...] - total * (STEP_SIZE / jnp.sqrt(mean + EPSILON))


def vmem(count):
    return [pl.BlockSpec(memory_space=pltpu.VMEM)] * count


def f32(*shape):
    return jax.ShapeDtypeStruct(shape, jnp.float32)


def moved(block, axis, distance):
    count = lax.axis_size(axis)
    return lax.ppermute(block, axis, [(i, (i + distance) % count) for i in range(count)])


LIMIT = pltpu.CompilerParams(vmem_limit_bytes=40 * 2**20)


def on_device(object_tiles, probe_modes, offsets, amplitude):
    rows, cols = object_tiles.shape[2:]
    ext_rows = rows + 2 * HALO
    scans = offsets.shape[2]
    tile = object_tiles.reshape(PLANES, rows, cols)
    flat_offsets = offsets.reshape(2 * scans)
    amp = amplitude.reshape(scans, WIN, WIN)

    north = moved(tile[:, rows - HALO :], "row", 1)
    south = moved(tile[:, :HALO], "row", -1)
    east_send, west_send = pl.pallas_call(
        pack_kernel,
        out_shape=[f32(ext_rows, LANES)] * 2,
        in_specs=vmem(3),
        out_specs=vmem(2),
    )(tile, north, south)
    from_west = moved(east_send, "col", 1)
    from_east = moved(west_send, "col", -1)

    probe_grad, core_grad, east_rim, west_rim = pl.pallas_call(
        main_kernel,
        out_shape=[f32(2, MODES, WIN, WIN), f32(PLANES, 2, ext_rows, LANES), f32(ext_rows, LANES), f32(ext_rows, LANES)],
        in_specs=[pl.BlockSpec(memory_space=pltpu.SMEM)] + vmem(8),
        out_specs=vmem(4),
        scratch_shapes=[
            pltpu.VMEM((PLANES, 4, ext_rows, LANES), jnp.float32),
            pltpu.VMEM((PLANES, 3, ext_rows, LANES), jnp.float32),
            pltpu.VMEM((MODES * WIN, 2 * WIN), jnp.bfloat16),
            pltpu.VMEM((MODES * WIN, 2 * WIN), jnp.bfloat16),
            pltpu.VMEM((2 * WIN, MODES * WIN), jnp.bfloat16),
            pltpu.VMEM((2 * WIN, MODES * WIN), jnp.bfloat16),
            pltpu.VMEM((2, MODES, WIN, WIN), jnp.float32),
            pltpu.VMEM((2, MODES, WIN, WIN), jnp.float32),
        ],
        compiler_params=LIMIT,
    )(flat_offsets, tile, north, south, from_west, from_east, probe_modes, amp, jnp.asarray(matrices()))

    rim_from_west = moved(east_rim, "col", 1)
    rim_from_east = moved(west_rim, "col", -1)
    devices = lax.axis_size("row") * lax.axis_size("col")
    parts = probe_grad.reshape(devices, -1, LANES)
    parts = lax.all_to_all(parts, BOTH, 0, 0, tiled=True)
    north_rim, south_rim, center, share = pl.pallas_call(
        middle_kernel,
        out_shape=[f32(PLANES, HALO, cols), f32(PLANES, HALO, cols), f32(PLANES, rows, cols), f32(*parts.shape)],
        in_specs=vmem(4),
        out_specs=vmem(4),
    )(core_grad, rim_from_west, rim_from_east, parts)
    from_south = moved(north_rim, "row", -1)
    from_north = moved(south_rim, "row", 1)
    total = lax.all_to_all(share, BOTH, 0, 0, tiled=True)
    object_grad, probe_new = pl.pallas_call(
        final_kernel,
        out_shape=[f32(PLANES, rows, cols), f32(2 * MODES * WIN, WIN)],
        in_specs=vmem(5),
        out_specs=vmem(2),
    )(center, from_north, from_south, total.reshape(2 * MODES * WIN, WIN), probe_modes.reshape(2 * MODES * WIN, WIN))
    return object_grad.reshape(object_tiles.shape), probe_new.reshape(probe_modes.shape)


def solution(mesh):
    placed = (
        P(None, None, "row", "col"),
        P(),
        P("row", "col", None, None),
        P("row", "col", None, None, None),
    )
    return jax.shard_map(
        on_device,
        mesh=mesh,
        in_specs=placed,
        out_specs=(P(None, None, "row", "col"), P()),
        check_vma=False,
    )
```

```python
import jax
import jax.numpy as jnp
import numpy as np
from jax import lax
from jax.experimental import pallas as pl
from jax.experimental.pallas import tpu as pltpu
from jax.sharding import PartitionSpec as P

HALO = 32
WIN = 128
MODES = 4
PLANES = 4
LANES = 128
PROP = 0.002
SHIFT_AMP = 0.5
STEP_SIZE = 0.5
EPSILON = 1e-06
BOTH = ("row", "col")


def matrices():
    k = np.arange(WIN)
    c = np.exp(-2j * np.pi * (np.outer(k, k) % WIN) / WIN) / np.sqrt(WIN)
    f = ((k + WIN // 2) % WIN - WIN // 2).astype(np.float64)
    g = c.conj() @ np.diag(np.exp(-1j * PROP * f * f)) @ c
    stack = []
    for m in (c, c.conj(), g, g.conj()):
        w = np.block([[m.real, m.imag], [-m.imag, m.real]]).astype(np.float32)
        high = w.astype(jnp.bfloat16)
        low = (w - high.astype(np.float32)).astype(jnp.bfloat16)
        stack.append(np.stack([high, low]))
    return np.stack(stack)


C, C_CONJ, G, G_CONJ = range(4)


def lane_iota(rows):
    return lax.broadcasted_iota(jnp.int32, (rows, LANES), 1)


def edges(src, rows):
    lane = lane_iota(rows)
    east = jnp.zeros((rows, LANES), jnp.float32)
    west = jnp.zeros((rows, LANES), jnp.float32)
    for p in range(PLANES):
        here = (lane >= p * HALO) & (lane < (p + 1) * HALO)
        east = jnp.where(here, turned(src[p, :, LANES : 2 * LANES], (p - 3) * HALO), east)
        west = jnp.where(here, turned(src[p, :, 0:LANES], p * HALO), west)
    return east, west


def turned(block, shift):
    return pltpu.roll(block, shift % LANES, 1) if shift % LANES else block


def pack_kernel(tile_ref, east_ref, west_ref):
    east_ref[...], west_ref[...] = edges(tile_ref, tile_ref.shape[1])


def corner_kernel(north_ref, south_ref, east_ref, west_ref):
    east_ref[0:HALO, :], west_ref[0:HALO, :] = edges(north_ref, HALO)
    east_ref[HALO:, :], west_ref[HALO:, :] = edges(south_ref, HALO)


def split(value):
    high = value.astype(jnp.bfloat16)
    return high, (value - high.astype(jnp.float32)).astype(jnp.bfloat16)


def dot(left, right):
    return jnp.dot(left, right, preferred_element_type=jnp.float32)


def main_kernel(
    offsets_ref, tile_ref, north_ref, south_ref, from_west_ref, from_east_ref, west_corners_ref, east_corners_ref,
    probe_ref, amp_ref, mat_ref,
    probe_grad_ref, center_ref, north_rim_ref, south_rim_ref, east_rim_ref, west_rim_ref,
    ext, grad, rh, rl, lh, ll, field, d_keep,
):
    rows = tile_ref.shape[1]
    ext_rows = rows + 2 * HALO
    last = HALO + rows
    lane_all = lane_iota(ext_rows)

    def beside(left, right, p):
        low = lane_iota(left.shape[0]) < 2 * HALO
        return jnp.where(low, turned(right, -p * HALO), turned(left, (3 - p) * HALO))

    for p in range(PLANES):
        for q in range(2):
            cols = slice(q * LANES, (q + 1) * LANES)
            ext[p, q, 0:HALO, :] = north_ref[p, :, cols]
            ext[p, q, HALO:last, :] = tile_ref[p, :, cols]
            ext[p, q, last:ext_rows, :] = south_ref[p, :, cols]
        ext[p, 2, 0:HALO, :] = beside(west_corners_ref[0:HALO, :], east_corners_ref[0:HALO, :], p)
        ext[p, 2, HALO:last, :] = beside(from_west_ref[...], from_east_ref[...], p)
        ext[p, 2, last:ext_rows, :] = beside(west_corners_ref[HALO:, :], east_corners_ref[HALO:, :], p)
        ext[p, 3, :, :] = ext[p, 0, :, :]
    grad[...] = jnp.zeros_like(grad)
    probe_grad_ref[...] = jnp.zeros_like(probe_grad_ref)

    lane = lane_iota(WIN)
    half = WIN

    def put_r(m, real, imag):
        h, l = split(real)
        rh[m * WIN : (m + 1) * WIN, 0:half] = h
        rl[m * WIN : (m + 1) * WIN, 0:half] = l
        h, l = split(imag)
        rh[m * WIN : (m + 1) * WIN, half:] = h
        rl[m * WIN : (m + 1) * WIN, half:] = l

    def put_l(m, real, imag):
        h, l = split(real)
        lh[0:half, m * WIN : (m + 1) * WIN] = h
        ll[0:half, m * WIN : (m + 1) * WIN] = l
        h, l = split(imag)
        lh[half:, m * WIN : (m + 1) * WIN] = h
        ll[half:, m * WIN : (m + 1) * WIN] = l

    def from_right(which):
        high, low = mat_ref[which, 0], mat_ref[which, 1]
        out = dot(rh[...], high) + dot(rl[...], high) + dot(rh[...], low)
        return [
            (out[m * WIN : (m + 1) * WIN, 0:half], out[m * WIN : (m + 1) * WIN, half:]) for m in range(MODES)
        ]

    def from_left(which):
        high, low = mat_ref[which ^ 1, 0], mat_ref[which ^ 1, 1]
        out = dot(high, lh[...]) + dot(high, ll[...]) + dot(low, lh[...])
        return [
            (out[0:half, m * WIN : (m + 1) * WIN], out[half:, m * WIN : (m + 1) * WIN]) for m in range(MODES)
        ]

    def scan_step(s, carry):
        row = offsets_ref[2 * s]
        start = lax.rem(offsets_ref[2 * s + 1] + (3 * LANES - HALO), 3 * LANES)
        q = lax.div(start, LANES)
        shift = lax.rem(start, LANES)
        back = lax.rem(LANES - shift, LANES)

        def window(p):
            a = pltpu.roll(ext[p, q, pl.ds(row, WIN), :], back, 1)
            b = pltpu.roll(ext[p, q + 1, pl.ds(row, WIN), :], back, 1)
            return jnp.where(lane < LANES - shift, a, b)

        def scatter(p, value):
            moved = pltpu.roll(value, shift, 1)
            grad[p, q, pl.ds(row, WIN), :] += jnp.where(lane >= shift, moved, 0.0)
            q2 = lax.rem(q + 1, 3)
            grad[p, q2, pl.ds(row, WIN), :] += jnp.where(lane < shift, moved, 0.0)

        first_r, second_r, first_i, second_i = (window(p) for p in range(PLANES))
        for m in range(MODES):
            pr, pi = probe_ref[0, m], probe_ref[1, m]
            put_r(m, pr * first_r - pi * first_i, pr * first_i + pi * first_r)
        for m, (real, imag) in enumerate(from_right(G)):
            put_l(m, real, imag)
        for m, (real, imag) in enumerate(from_left(G)):
            d_keep[0, m] = real
            d_keep[1, m] = imag
            put_l(m, real * second_r - imag * second_i, real * second_i + imag * second_r)
        for m, (real, imag) in enumerate(from_left(C)):
            put_r(m, real, imag)
        intensity = jnp.full((WIN, WIN), SHIFT_AMP, jnp.float32)
        for m, (real, imag) in enumerate(from_right(C)):
            field[0, m] = real
            field[1, m] = imag
            intensity = intensity + (real * real + imag * imag)
        factor = 2.0 - 2.0 * amp_ref[s] / jnp.sqrt(intensity)
        for m in range(MODES):
            put_r(m, field[0, m] * factor, field[1, m] * factor)
        for m, (real, imag) in enumerate(from_right(C_CONJ)):
            put_l(m, real, imag)
        sum_r = jnp.zeros((WIN, WIN), jnp.float32)
        sum_i = jnp.zeros((WIN, WIN), jnp.float32)
        for m, (real, imag) in enumerate(from_left(C_CONJ)):
            dr, di = d_keep[0, m], d_keep[1, m]
            sum_r = sum_r + (dr * real + di * imag)
            sum_i = sum_i + (dr * imag - di * real)
            put_l(m, second_r * real + second_i * imag, second_r * imag - second_i * real)
        scatter(1, sum_r)
        scatter(3, sum_i)
        for m, (real, imag) in enumerate(from_left(G_CONJ)):
            put_r(m, real, imag)
        sum_r = jnp.zeros((WIN, WIN), jnp.float32)
        sum_i = jnp.zeros((WIN, WIN), jnp.float32)
        for m, (real, imag) in enumerate(from_right(G_CONJ)):
            pr, pi = probe_ref[0, m], probe_ref[1, m]
            sum_r = sum_r + (pr * real + pi * imag)
            sum_i = sum_i + (pr * imag - pi * real)
            probe_grad_ref[0, m] += first_r * real + first_i * imag
            probe_grad_ref[1, m] += first_r * imag - first_i * real
        scatter(0, sum_r)
        scatter(2, sum_i)
        return carry

    lax.fori_loop(0, amp_ref.shape[0], scan_step, 0)

    east = jnp.zeros((ext_rows, LANES), jnp.float32)
    west = jnp.zeros((ext_rows, LANES), jnp.float32)
    for p in range(PLANES):
        for q in range(2):
            cols = slice(q * LANES, (q + 1) * LANES)
            north_rim_ref[p, :, cols] = grad[p, q, 0:HALO, :]
            center_ref[p, :, cols] = grad[p, q, HALO:last, :]
            south_rim_ref[p, :, cols] = grad[p, q, last:ext_rows, :]
        third = grad[p, 2]
        here = (lane_all >= p * HALO) & (lane_all < (p + 1) * HALO)
        east = jnp.where(here, turned(third, p * HALO), east)
        west = jnp.where(here, turned(third, (p - 3) * HALO), west)
    east_rim_ref[...] = east
    west_rim_ref[...] = west


def share_kernel(parts_ref, share_ref):
    share_ref[...] = jnp.broadcast_to(jnp.sum(parts_ref[...], axis=0)[None], share_ref.shape)


def object_kernel(
    center_ref, from_north_ref, from_south_ref, from_west_ref, from_east_ref, north_corners_ref, south_corners_ref,
    object_ref,
):
    rows = center_ref.shape[1]

    def rim(left, right, p):
        lane = lane_iota(left.shape[0])
        return (
            jnp.where(lane < HALO, turned(left, -p * HALO), 0.0),
            jnp.where(lane >= LANES - HALO, turned(right, (3 - p) * HALO), 0.0),
        )

    for p in range(PLANES):
        sides = rim(from_west_ref[HALO : HALO + rows, :], from_east_ref[HALO : HALO + rows, :], p)
        north = rim(north_corners_ref[0:HALO, :], north_corners_ref[HALO:, :], p)
        south = rim(south_corners_ref[0:HALO, :], south_corners_ref[HALO:, :], p)
        for q in range(2):
            cols = slice(q * LANES, (q + 1) * LANES)
            whole = center_ref[p, :, cols] + sides[q]
            object_ref[p, 0:HALO, cols] = whole[0:HALO] + from_north_ref[p, :, cols] + north[q]
            object_ref[p, HALO : rows - HALO, cols] = whole[HALO : rows - HALO]
            object_ref[p, rows - HALO :, cols] = whole[rows - HALO :] + from_south_ref[p, :, cols] + south[q]


def probe_kernel(total_ref, probe_ref, probe_new_ref):
    total = total_ref[...]
    squares = jnp.sum(total * total, axis=0, keepdims=True)
    mean = jnp.sum(squares, axis=1, keepdims=True) / (total.shape[0] * total.shape[1])
    probe_new_ref[...] = probe_ref[...] - total * (STEP_SIZE / jnp.sqrt(mean + EPSILON))


def vmem(count):
    return [pl.BlockSpec(memory_space=pltpu.VMEM)] * count


def f32(*shape):
    return jax.ShapeDtypeStruct(shape, jnp.float32)


def moved(block, axis, distance):
    count = lax.axis_size(axis)
    return lax.ppermute(block, axis, [(i, (i + distance) % count) for i in range(count)])


def call(kernel, outs, ins, scratch=(), scalars=0, limit=2):
    return pl.pallas_call(
        kernel,
        out_shape=outs,
        in_specs=[pl.BlockSpec(memory_space=pltpu.SMEM)] * scalars + vmem(ins),
        out_specs=vmem(len(outs)) if isinstance(outs, list) else vmem(1)[0],
        scratch_shapes=scratch,
        compiler_params=pltpu.CompilerParams(vmem_limit_bytes=limit * 2**20),
    )


def on_device(object_tiles, probe_modes, offsets, amplitude):
    rows, cols = object_tiles.shape[2:]
    ext_rows = rows + 2 * HALO
    scans = offsets.shape[2]
    tile = object_tiles.reshape(PLANES, rows, cols)
    flat_offsets = offsets.reshape(2 * scans)
    amp = amplitude.reshape(scans, WIN, WIN)
    flat = (2 * MODES * WIN, WIN)
    devices = lax.axis_size("row") * lax.axis_size("col")

    north = moved(tile[:, rows - HALO :], "row", 1)
    south = moved(tile[:, :HALO], "row", -1)
    east_send, west_send = call(pack_kernel, [f32(rows, LANES)] * 2, 1)(tile)
    from_west = moved(east_send, "col", 1)
    from_east = moved(west_send, "col", -1)
    east_send, west_send = call(corner_kernel, [f32(2 * HALO, LANES)] * 2, 2)(north, south)
    west_corners = moved(east_send, "col", 1)
    east_corners = moved(west_send, "col", -1)

    pair = pltpu.VMEM((MODES * WIN, 2 * WIN), jnp.bfloat16)
    wide = pltpu.VMEM((2 * WIN, MODES * WIN), jnp.bfloat16)
    modes = pltpu.VMEM((2, MODES, WIN, WIN), jnp.float32)
    probe_grad, center, north_rim, south_rim, east_rim, west_rim = call(
        main_kernel,
        [f32(2, MODES, WIN, WIN), f32(PLANES, rows, cols)]
        + [f32(PLANES, HALO, cols)] * 2
        + [f32(ext_rows, LANES)] * 2,
        10,
        [
            pltpu.VMEM((PLANES, 4, ext_rows, LANES), jnp.float32),
            pltpu.VMEM((PLANES, 3, ext_rows, LANES), jnp.float32),
            pair, pair, wide, wide, modes, modes,
        ],
        scalars=1,
        limit=16,
    )(
        flat_offsets, tile, north, south, from_west, from_east, west_corners, east_corners,
        probe_modes, amp, jnp.asarray(matrices()),
    )

    parts = lax.all_to_all(probe_grad.reshape(devices, -1, LANES), BOTH, 0, 0, tiled=True)
    rim_from_west = moved(east_rim, "col", 1)
    rim_from_east = moved(west_rim, "col", -1)
    from_south = moved(north_rim, "row", -1)
    from_north = moved(south_rim, "row", 1)
    share = call(share_kernel, f32(*parts.shape), 1)(parts)
    total = lax.all_to_all(share, BOTH, 0, 0, tiled=True)
    sides = (rim_from_west, rim_from_east)
    south_corners = moved(jnp.concatenate([side[:HALO] for side in sides]), "row", -1)
    north_corners = moved(jnp.concatenate([side[ext_rows - HALO :] for side in sides]), "row", 1)
    object_grad = call(object_kernel, f32(PLANES, rows, cols), 7)(
        center, from_north, from_south, rim_from_west, rim_from_east, north_corners, south_corners
    )
    probe_new = call(probe_kernel, f32(*flat), 2)(total.reshape(flat), probe_modes.reshape(flat))
    return object_grad.reshape(object_tiles.shape), probe_new.reshape(probe_modes.shape)


def solution(mesh):
    placed = (
        P(None, None, "row", "col"),
        P(),
        P("row", "col", None, None),
        P("row", "col", None, None, None),
    )
    return jax.shard_map(
        on_device,
        mesh=mesh,
        in_specs=placed,
        out_specs=(P(None, None, "row", "col"), P()),
        check_vma=False,
    )
```

```python
import jax
import jax.numpy as jnp
import numpy as np
from jax import lax
from jax.experimental import pallas as pl
from jax.experimental.pallas import tpu as pltpu
from jax.sharding import PartitionSpec as P

HALO = 32
WIN = 128
MODES = 4
PLANES = 4
LANES = 128
PROP = 0.002
SHIFT_AMP = 0.5
STEP_SIZE = 0.5
EPSILON = 1e-06
BOTH = ("row", "col")


def matrices():
    k = np.arange(WIN)
    c = np.exp(-2j * np.pi * (np.outer(k, k) % WIN) / WIN) / np.sqrt(WIN)
    f = ((k + WIN // 2) % WIN - WIN // 2).astype(np.float64)
    g = c.conj() @ np.diag(np.exp(-1j * PROP * f * f)) @ c
    stack = []
    for m in (c, c.conj(), g, g.conj()):
        w = np.block([[m.real, m.imag], [-m.imag, m.real]]).astype(np.float32)
        high = w.astype(jnp.bfloat16)
        low = (w - high.astype(np.float32)).astype(jnp.bfloat16)
        stack.append(np.stack([high, low]))
    return np.stack(stack)


C, C_CONJ, G, G_CONJ = range(4)


def lane_iota(rows):
    return lax.broadcasted_iota(jnp.int32, (rows, LANES), 1)


def edges(src, rows):
    lane = lane_iota(rows)
    east = jnp.zeros((rows, LANES), jnp.float32)
    west = jnp.zeros((rows, LANES), jnp.float32)
    for p in range(PLANES):
        here = (lane >= p * HALO) & (lane < (p + 1) * HALO)
        east = jnp.where(here, turned(src[p, :, LANES : 2 * LANES], (p - 3) * HALO), east)
        west = jnp.where(here, turned(src[p, :, 0:LANES], p * HALO), west)
    return east, west


def turned(block, shift):
    return pltpu.roll(block, shift % LANES, 1) if shift % LANES else block


def pack_kernel(tile_ref, east_ref, west_ref):
    east_ref[...], west_ref[...] = edges(tile_ref, tile_ref.shape[1])


def corner_kernel(north_ref, south_ref, east_ref, west_ref):
    east_ref[0:HALO, :], west_ref[0:HALO, :] = edges(north_ref, HALO)
    east_ref[HALO:, :], west_ref[HALO:, :] = edges(south_ref, HALO)


def split(value):
    high = value.astype(jnp.bfloat16)
    return high, (value - high.astype(jnp.float32)).astype(jnp.bfloat16)


def dot(left, right):
    return jnp.dot(left, right, preferred_element_type=jnp.float32)


def assemble_kernel(tile_ref, north_ref, south_ref, ext):
    rows = tile_ref.shape[1]
    for p in range(PLANES):
        for q in range(2):
            cols = slice(q * LANES, (q + 1) * LANES)
            ext[p, q, 0:HALO, :] = north_ref[p, :, cols]
            ext[p, q, HALO : HALO + rows, :] = tile_ref[p, :, cols]
            ext[p, q, HALO + rows :, :] = south_ref[p, :, cols]


def place(offsets_ref, s, q_count=3):
    start = lax.rem(offsets_ref[2 * s + 1] + (q_count * LANES - HALO), q_count * LANES)
    first = lax.div(start, LANES)
    return offsets_ref[2 * s], first, lax.rem(first + 1, q_count), lax.rem(start, LANES)


def main_kernel(
    offsets_ref, ext_in, from_west_ref, from_east_ref, west_corners_ref, east_corners_ref, amp_ref, probe_ref, mat_ref,
    probe_grad_ref, window_grad_ref, ext,
    rh, rl, lh, ll, field, d_keep, win,
):
    del ext_in
    ext_rows = ext.shape[2]
    last = ext_rows - HALO

    def beside(left, right, p):
        low = lane_iota(left.shape[0]) < 2 * HALO
        return jnp.where(low, turned(right, -p * HALO), turned(left, (3 - p) * HALO))

    for p in range(PLANES):
        ext[p, 2, 0:HALO, :] = beside(west_corners_ref[0:HALO, :], east_corners_ref[0:HALO, :], p)
        ext[p, 2, HALO:last, :] = beside(from_west_ref[...], from_east_ref[...], p)
        ext[p, 2, last:ext_rows, :] = beside(west_corners_ref[HALO:, :], east_corners_ref[HALO:, :], p)
    probe_grad_ref[...] = jnp.zeros_like(probe_grad_ref)

    lane = lane_iota(WIN)
    chains = range(MODES // 2)

    def put(high, low, at, value):
        high[at], low[at] = split(value)

    def put_r(c, k, real, imag):
        rows = slice(k * WIN, (k + 1) * WIN)
        put(rh, rl, (c, rows, slice(0, WIN)), real)
        put(rh, rl, (c, rows, slice(WIN, 2 * WIN)), imag)

    def put_l(c, k, real, imag):
        cols = slice(k * WIN, (k + 1) * WIN)
        put(lh, ll, (c, slice(0, WIN), cols), real)
        put(lh, ll, (c, slice(WIN, 2 * WIN), cols), imag)

    def from_right(which):
        for c in chains:
            high, low = mat_ref[which, 0], mat_ref[which, 1]
            out = dot(jnp.concatenate([rh[c], rl[c], rh[c]], axis=1), jnp.concatenate([high, high, low], axis=0))
            for k in range(2):
                rows = slice(k * WIN, (k + 1) * WIN)
                yield c, k, out[rows, 0:WIN], out[rows, WIN:]

    def from_left(which):
        for c in chains:
            high, low = mat_ref[which ^ 1, 0], mat_ref[which ^ 1, 1]
            out = dot(jnp.concatenate([high, high, low], axis=1), jnp.concatenate([lh[c], ll[c], lh[c]], axis=0))
            for k in range(2):
                cols = slice(k * WIN, (k + 1) * WIN)
                yield c, k, out[0:WIN, cols], out[WIN:, cols]

    def scan_step(s, carry):
        row, q, q_next, shift = place(offsets_ref, s)
        back = lax.rem(LANES - shift, LANES)

        def window(p):
            a = pltpu.roll(ext[p, q, pl.ds(row, WIN), :], back, 1)
            b = pltpu.roll(ext[p, q_next, pl.ds(row, WIN), :], back, 1)
            return jnp.where(lane < LANES - shift, a, b)

        for p in range(PLANES):
            win[p] = window(p)
        for c in chains:
            for k in range(2):
                pr, pi = probe_ref[0, 2 * c + k], probe_ref[1, 2 * c + k]
                put_r(c, k, pr * win[0] - pi * win[2], pr * win[2] + pi * win[0])
        for c, k, real, imag in from_right(G):
            put_l(c, k, real, imag)
        for c, k, real, imag in from_left(G):
            m = 2 * c + k
            d_keep[0, m] = real
            d_keep[1, m] = imag
            put_l(c, k, real * win[1] - imag * win[3], real * win[3] + imag * win[1])
        for c, k, real, imag in from_left(C):
            put_r(c, k, real, imag)
        intensity = jnp.full((WIN, WIN), SHIFT_AMP, jnp.float32)
        for c, k, real, imag in from_right(C):
            m = 2 * c + k
            field[0, m] = real
            field[1, m] = imag
            intensity = intensity + (real * real + imag * imag)
        factor = 2.0 - 2.0 * amp_ref[s] / jnp.sqrt(intensity)
        for c in chains:
            for k in range(2):
                m = 2 * c + k
                put_r(c, k, field[0, m] * factor, field[1, m] * factor)
        for c, k, real, imag in from_right(C_CONJ):
            put_l(c, k, real, imag)
        sum_r = jnp.zeros((WIN, WIN), jnp.float32)
        sum_i = jnp.zeros((WIN, WIN), jnp.float32)
        for c, k, real, imag in from_left(C_CONJ):
            dr, di = d_keep[0, 2 * c + k], d_keep[1, 2 * c + k]
            sum_r = sum_r + (dr * real + di * imag)
            sum_i = sum_i + (dr * imag - di * real)
            put_l(c, k, win[1] * real + win[3] * imag, win[1] * imag - win[3] * real)
        window_grad_ref[s, 1] = sum_r
        window_grad_ref[s, 3] = sum_i
        for c, k, real, imag in from_left(G_CONJ):
            put_r(c, k, real, imag)
        sum_r = jnp.zeros((WIN, WIN), jnp.float32)
        sum_i = jnp.zeros((WIN, WIN), jnp.float32)
        for c, k, real, imag in from_right(G_CONJ):
            m = 2 * c + k
            pr, pi = probe_ref[0, m], probe_ref[1, m]
            sum_r = sum_r + (pr * real + pi * imag)
            sum_i = sum_i + (pr * imag - pi * real)
            probe_grad_ref[0, m] += win[0] * real + win[2] * imag
            probe_grad_ref[1, m] += win[0] * imag - win[2] * real
        window_grad_ref[s, 0] = sum_r
        window_grad_ref[s, 2] = sum_i
        return carry

    lax.fori_loop(0, amp_ref.shape[0], scan_step, 0)


def scatter_kernel(offsets_ref, window_grad_ref, center_ref, north_rim_ref, south_rim_ref, east_rim_ref, west_rim_ref, grad):
    grad[...] = jnp.zeros_like(grad)
    lane = lane_iota(WIN)
    for s in range(window_grad_ref.shape[0]):
        row, q, q_next, shift = place(offsets_ref, s)
        for p in range(PLANES):
            value = pltpu.roll(window_grad_ref[s, p], shift, 1)
            grad[p, q, pl.ds(row, WIN), :] += jnp.where(lane >= shift, value, 0.0)
            grad[p, q_next, pl.ds(row, WIN), :] += jnp.where(lane < shift, value, 0.0)
    ext_rows = grad.shape[2]
    last = ext_rows - HALO
    lane = lane_iota(ext_rows)
    east = jnp.zeros((ext_rows, LANES), jnp.float32)
    west = jnp.zeros((ext_rows, LANES), jnp.float32)
    for p in range(PLANES):
        for q in range(2):
            cols = slice(q * LANES, (q + 1) * LANES)
            north_rim_ref[p, :, cols] = grad[p, q, 0:HALO, :]
            center_ref[p, :, cols] = grad[p, q, HALO:last, :]
            south_rim_ref[p, :, cols] = grad[p, q, last:ext_rows, :]
        third = grad[p, 2]
        here = (lane >= p * HALO) & (lane < (p + 1) * HALO)
        east = jnp.where(here, turned(third, p * HALO), east)
        west = jnp.where(here, turned(third, (p - 3) * HALO), west)
    east_rim_ref[...] = east
    west_rim_ref[...] = west


def rim_corner_kernel(from_west_ref, from_east_ref, to_north_ref, to_south_ref):
    for k, ref in enumerate((from_west_ref, from_east_ref)):
        to_north_ref[k * HALO : (k + 1) * HALO, :] = ref[0:HALO, :]
        to_south_ref[k * HALO : (k + 1) * HALO, :] = ref[ref.shape[0] - HALO :, :]


def share_kernel(parts_ref, from_west_ref, from_east_ref, share_ref):
    del from_west_ref, from_east_ref
    share_ref[...] = jnp.broadcast_to(jnp.sum(parts_ref[...], axis=0)[None], share_ref.shape)


def object_kernel(
    center_ref, from_north_ref, from_south_ref, from_west_ref, from_east_ref, north_corners_ref, south_corners_ref,
    object_ref,
):
    rows = center_ref.shape[1]

    def rim(left, right, p):
        lane = lane_iota(left.shape[0])
        return (
            jnp.where(lane < HALO, turned(left, -p * HALO), 0.0),
            jnp.where(lane >= LANES - HALO, turned(right, (3 - p) * HALO), 0.0),
        )

    for p in range(PLANES):
        sides = rim(from_west_ref[HALO : HALO + rows, :], from_east_ref[HALO : HALO + rows, :], p)
        north = rim(north_corners_ref[0:HALO, :], north_corners_ref[HALO:, :], p)
        south = rim(south_corners_ref[0:HALO, :], south_corners_ref[HALO:, :], p)
        for q in range(2):
            cols = slice(q * LANES, (q + 1) * LANES)
            whole = center_ref[p, :, cols] + sides[q]
            object_ref[p, 0:HALO, cols] = whole[0:HALO] + from_north_ref[p, :, cols] + north[q]
            object_ref[p, HALO : rows - HALO, cols] = whole[HALO : rows - HALO]
            object_ref[p, rows - HALO :, cols] = whole[rows - HALO :] + from_south_ref[p, :, cols] + south[q]


def probe_kernel(total_ref, probe_ref, probe_new_ref):
    total = total_ref[...]
    squares = jnp.sum(total * total, axis=0, keepdims=True)
    mean = jnp.sum(squares, axis=1, keepdims=True) / (total.shape[0] * total.shape[1])
    probe_new_ref[...] = probe_ref[...] - total * (STEP_SIZE / jnp.sqrt(mean + EPSILON))


def vmem(count):
    return [pl.BlockSpec(memory_space=pltpu.VMEM)] * count


def f32(*shape):
    return jax.ShapeDtypeStruct(shape, jnp.float32)


def moved(block, axis, distance):
    count = lax.axis_size(axis)
    return lax.ppermute(block, axis, [(i, (i + distance) % count) for i in range(count)])


def cost(us):
    return pl.CostEstimate(flops=int(us * 1e9), bytes_accessed=int(us * 3e6), transcendentals=0)


def call(kernel, outs, ins, scratch=(), scalars=0, limit=2, us=1):
    return pl.pallas_call(
        kernel,
        out_shape=outs,
        in_specs=[pl.BlockSpec(memory_space=pltpu.SMEM)] * scalars + vmem(ins),
        out_specs=vmem(len(outs)) if isinstance(outs, list) else vmem(1)[0],
        scratch_shapes=scratch,
        compiler_params=pltpu.CompilerParams(vmem_limit_bytes=limit * 2**20),
        cost_estimate=cost(us),
    )


def main_call(scans, ext_rows):
    pair = pltpu.VMEM((MODES // 2, 2 * WIN, 2 * WIN), jnp.bfloat16)
    modes = pltpu.VMEM((2, MODES, WIN, WIN), jnp.float32)
    run = pl.pallas_call(
        main_kernel,
        out_shape=[f32(2, MODES, WIN, WIN), f32(scans, PLANES, WIN, WIN), f32(PLANES, 3, ext_rows, LANES)],
        in_specs=[pl.BlockSpec(memory_space=pltpu.SMEM)] + vmem(8),
        out_specs=vmem(3),
        scratch_shapes=[
            pair, pair, pair, pair, modes, modes,
            pltpu.VMEM((PLANES, WIN, WIN), jnp.float32),
        ],
        input_output_aliases={1: 2},
        compiler_params=pltpu.CompilerParams(vmem_limit_bytes=12 * 2**20),
        cost_estimate=cost(12),
    )
    return lambda *args: run(*args)[:2]


def on_device(object_tiles, probe_modes, offsets, amplitude):
    rows, cols = object_tiles.shape[2:]
    ext_rows = rows + 2 * HALO
    scans = offsets.shape[2]
    tile = object_tiles.reshape(PLANES, rows, cols)
    tile, flat_offsets = lax.optimization_barrier((tile, offsets.reshape(2 * scans)))
    amp = amplitude.reshape(scans, WIN, WIN)
    flat = (2 * MODES * WIN, WIN)
    mats = jnp.asarray(matrices())
    devices = lax.axis_size("row") * lax.axis_size("col")

    north = moved(tile[:, rows - HALO :], "row", 1)
    south = moved(tile[:, :HALO], "row", -1)
    east_send, west_send = call(pack_kernel, [f32(rows, LANES)] * 2, 1)(tile)
    from_west = moved(east_send, "col", 1)
    from_east = moved(west_send, "col", -1)
    east_send, west_send = call(corner_kernel, [f32(2 * HALO, LANES)] * 2, 2)(north, south)
    west_corners = moved(east_send, "col", 1)
    east_corners = moved(west_send, "col", -1)

    ext = call(assemble_kernel, f32(PLANES, 3, ext_rows, LANES), 3, us=4)(tile, north, south)
    probe_grad, window_grad = main_call(scans, ext_rows)(
        flat_offsets, ext, from_west, from_east, west_corners, east_corners, amp, probe_modes, mats
    )
    center, north_rim, south_rim, east_rim, west_rim = call(
        scatter_kernel,
        [f32(PLANES, rows, cols)] + [f32(PLANES, HALO, cols)] * 2 + [f32(ext_rows, LANES)] * 2,
        1,
        [pltpu.VMEM((PLANES, 3, ext_rows, LANES), jnp.float32)],
        scalars=1,
        limit=6,
    )(flat_offsets, window_grad)

    parts = lax.all_to_all(probe_grad.reshape(devices, -1, LANES), BOTH, 0, 0, tiled=True)
    rim_from_west = moved(east_rim, "col", 1)
    rim_from_east = moved(west_rim, "col", -1)
    from_south = moved(north_rim, "row", -1)
    from_north = moved(south_rim, "row", 1)
    share = call(share_kernel, f32(*parts.shape), 3)(parts, rim_from_west, rim_from_east)
    total = lax.all_to_all(share, BOTH, 0, 0, tiled=True)
    to_north, to_south = call(rim_corner_kernel, [f32(2 * HALO, LANES)] * 2, 2)(rim_from_west, rim_from_east)
    south_corners = moved(to_north, "row", -1)
    north_corners = moved(to_south, "row", 1)
    object_grad = call(object_kernel, f32(PLANES, rows, cols), 7)(
        center, from_north, from_south, rim_from_west, rim_from_east, north_corners, south_corners
    )
    probe_new = call(probe_kernel, f32(*flat), 2)(total.reshape(flat), probe_modes.reshape(flat))
    return object_grad.reshape(object_tiles.shape), probe_new.reshape(probe_modes.shape)


def solution(mesh):
    placed = (
        P(None, None, "row", "col"),
        P(),
        P("row", "col", None, None),
        P("row", "col", None, None, None),
    )
    return jax.shard_map(
        on_device,
        mesh=mesh,
        in_specs=placed,
        out_specs=(P(None, None, "row", "col"), P()),
        check_vma=False,
    )
```

```python
import jax
import jax.numpy as jnp
import numpy as np
from jax import lax
from jax.experimental import pallas as pl
from jax.experimental.pallas import tpu as pltpu
from jax.sharding import PartitionSpec as P

HALO = 32
WIN = 128
MODES = 4
PLANES = 4
LANES = 128
PROP = 0.002
SHIFT_AMP = 0.5
STEP_SIZE = 0.5
EPSILON = 1e-06
BOTH = ("row", "col")


def matrices():
    k = np.arange(WIN)
    c = np.exp(-2j * np.pi * (np.outer(k, k) % WIN) / WIN) / np.sqrt(WIN)
    f = ((k + WIN // 2) % WIN - WIN // 2).astype(np.float64)
    g = c.conj() @ np.diag(np.exp(-1j * PROP * f * f)) @ c
    stack = []
    for m in (c, c.conj(), g, g.conj()):
        w = np.block([[m.real, m.imag], [-m.imag, m.real]]).astype(np.float32)
        high = w.astype(jnp.bfloat16)
        low = (w - high.astype(np.float32)).astype(jnp.bfloat16)
        stack.append(np.stack([high, low]))
    return np.stack(stack)


C, C_CONJ, G, G_CONJ = range(4)
BLOCKS = 2
ROWS = 2 * WIN // BLOCKS


def lane_iota(rows):
    return lax.broadcasted_iota(jnp.int32, (rows, LANES), 1)


def edges(src, rows):
    lane = lane_iota(rows)
    east = jnp.zeros((rows, LANES), jnp.float32)
    west = jnp.zeros((rows, LANES), jnp.float32)
    for p in range(PLANES):
        here = (lane >= p * HALO) & (lane < (p + 1) * HALO)
        east = jnp.where(here, turned(src[p, :, LANES : 2 * LANES], (p - 3) * HALO), east)
        west = jnp.where(here, turned(src[p, :, 0:LANES], p * HALO), west)
    return east, west


def turned(block, shift):
    return pltpu.roll(block, shift % LANES, 1) if shift % LANES else block


def pack_kernel(tile_ref, east_ref, west_ref):
    east_ref[...], west_ref[...] = edges(tile_ref, tile_ref.shape[1])


def corner_kernel(north_ref, south_ref, east_ref, west_ref):
    east_ref[0:HALO, :], west_ref[0:HALO, :] = edges(north_ref, HALO)
    east_ref[HALO:, :], west_ref[HALO:, :] = edges(south_ref, HALO)


def split(value):
    high = value.astype(jnp.bfloat16)
    return high, (value - high.astype(jnp.float32)).astype(jnp.bfloat16)


def dot(left, right):
    return jnp.dot(left, right, preferred_element_type=jnp.float32)


def assemble_kernel(tile_ref, north_ref, south_ref, ext):
    rows = tile_ref.shape[1]
    for p in range(PLANES):
        for q in range(2):
            cols = slice(q * LANES, (q + 1) * LANES)
            ext[p, q, 0:HALO, :] = north_ref[p, :, cols]
            ext[p, q, HALO : HALO + rows, :] = tile_ref[p, :, cols]
            ext[p, q, HALO + rows :, :] = south_ref[p, :, cols]


def place(offsets_ref, s, q_count=3):
    start = lax.rem(offsets_ref[1, s] + (q_count * LANES - HALO), q_count * LANES)
    first = lax.div(start, LANES)
    return offsets_ref[0, s], first, lax.rem(first + 1, q_count), lax.rem(start, LANES)


def main_kernel(
    offsets_ref, ext_in, from_west_ref, from_east_ref, west_corners_ref, east_corners_ref, amp_ref, probe_ref, mat_ref,
    probe_grad_ref, center_ref, north_rim_ref, south_rim_ref, east_rim_ref, west_rim_ref, ext,
    rh, rl, lh, ll, field, d_keep, win, factor, grad,
):
    del ext_in
    ext_rows = ext.shape[2]
    last = ext_rows - HALO

    def beside(left, right, p):
        low = lane_iota(left.shape[0]) < 2 * HALO
        return jnp.where(low, turned(right, -p * HALO), turned(left, (3 - p) * HALO))

    for p in range(PLANES):
        ext[p, 2, 0:HALO, :] = beside(west_corners_ref[0:HALO, :], east_corners_ref[0:HALO, :], p)
        ext[p, 2, HALO:last, :] = beside(from_west_ref[...], from_east_ref[...], p)
        ext[p, 2, last:ext_rows, :] = beside(west_corners_ref[HALO:, :], east_corners_ref[HALO:, :], p)

    lane = lane_iota(WIN)
    chains = range(MODES // 2)
    scans = range(amp_ref.shape[0])

    def put(high, low, at, value):
        high[at], low[at] = split(value)

    def run(*accs):
        def blocks(s, c):
            first = (s * len(chains) + c) * BLOCKS
            return accs[first : first + BLOCKS]

        def multiply(s, c, rhs, lhss, stage):
            pltpu.matmul_push_rhs(rhs, stage, c)
            for lhs in lhss:
                for b, acc in enumerate(blocks(s, c)):
                    pltpu.matmul_acc_lhs(acc, lhs[b * ROWS : (b + 1) * ROWS, :], stage)
                    stage = None

        def start_right(s, which):
            for c in chains:
                multiply(s, c, mat_ref[which, 0], (rh[s, c], rl[s, c]), 0)
                multiply(s, c, mat_ref[which, 1], (rh[s, c],), 1)

        def start_left(s, which):
            high, low = mat_ref[which ^ 1, 0], mat_ref[which ^ 1, 1]
            for c in chains:
                multiply(s, c, lh[s, c], (high, low), 0)
                multiply(s, c, ll[s, c], (high,), 1)

        def planes_right(s):
            for c in chains:
                out = jnp.concatenate([pltpu.matmul_pop(acc) for acc in blocks(s, c)], axis=0)
                for k in range(2):
                    yield c, k, out[k * WIN : (k + 1) * WIN, 0:WIN], out[k * WIN : (k + 1) * WIN, WIN:]

        def planes_left(s):
            for c in chains:
                out = jnp.concatenate([pltpu.matmul_pop(acc) for acc in blocks(s, c)], axis=0)
                for k in range(2):
                    yield c, k, out[0:WIN, k * WIN : (k + 1) * WIN], out[WIN:, k * WIN : (k + 1) * WIN]

        def put_r(s, c, k, real, imag):
            rows = slice(k * WIN, (k + 1) * WIN)
            put(rh, rl, (s, c, rows, slice(0, WIN)), real)
            put(rh, rl, (s, c, rows, slice(WIN, 2 * WIN)), imag)

        def put_l(s, c, k, real, imag):
            cols = slice(k * WIN, (k + 1) * WIN)
            put(lh, ll, (s, c, slice(0, WIN), cols), real)
            put(lh, ll, (s, c, slice(WIN, 2 * WIN), cols), imag)

        def steps(s):
            row, q, q_next, shift = place(offsets_ref, s)
            back = lax.rem(LANES - shift, LANES)

            def scatter(p, value):
                value = pltpu.roll(value, shift, 1)
                grad[p, q, pl.ds(row, WIN), :] += jnp.where(lane >= shift, value, 0.0)
                grad[p, q_next, pl.ds(row, WIN), :] += jnp.where(lane < shift, value, 0.0)

            for p in range(PLANES):
                a = pltpu.roll(ext[p, q, pl.ds(row, WIN), :], back, 1)
                b = pltpu.roll(ext[p, q_next, pl.ds(row, WIN), :], back, 1)
                win[s, p] = jnp.where(lane < LANES - shift, a, b)
            for c in chains:
                for k in range(2):
                    pr, pi = probe_ref[0, 2 * c + k], probe_ref[1, 2 * c + k]
                    put_r(s, c, k, pr * win[s, 0] - pi * win[s, 2], pr * win[s, 2] + pi * win[s, 0])
            start_right(s, G)
            if s == 0:
                grad[...] = jnp.zeros_like(grad)
            yield
            for c, k, real, imag in planes_right(s):
                put_l(s, c, k, real, imag)
            start_left(s, G)
            yield
            for c, k, real, imag in planes_left(s):
                m = 2 * c + k
                d_keep[s, 0, m] = real
                d_keep[s, 1, m] = imag
                second_r, second_i = win[s, 1], win[s, 3]
                put_l(s, c, k, real * second_r - imag * second_i, real * second_i + imag * second_r)
            start_left(s, C)
            yield
            for c, k, real, imag in planes_left(s):
                put_r(s, c, k, real, imag)
            start_right(s, C)
            yield
            intensity = jnp.full((WIN, WIN), SHIFT_AMP, jnp.float32)
            for c, k, real, imag in planes_right(s):
                m = 2 * c + k
                field[s, 0, m] = real
                field[s, 1, m] = imag
                intensity = intensity + (real * real + imag * imag)
            factor[s] = 2.0 - 2.0 * amp_ref[s] / jnp.sqrt(intensity)
            for c in chains:
                for k in range(2):
                    m = 2 * c + k
                    put_r(s, c, k, field[s, 0, m] * factor[s], field[s, 1, m] * factor[s])
            start_right(s, C_CONJ)
            yield
            for c, k, real, imag in planes_right(s):
                put_l(s, c, k, real, imag)
            start_left(s, C_CONJ)
            yield
            sum_r = jnp.zeros((WIN, WIN), jnp.float32)
            sum_i = jnp.zeros((WIN, WIN), jnp.float32)
            for c, k, real, imag in planes_left(s):
                dr, di = d_keep[s, 0, 2 * c + k], d_keep[s, 1, 2 * c + k]
                second_r, second_i = win[s, 1], win[s, 3]
                sum_r = sum_r + (dr * real + di * imag)
                sum_i = sum_i + (dr * imag - di * real)
                put_l(s, c, k, second_r * real + second_i * imag, second_r * imag - second_i * real)
            start_left(s, G_CONJ)
            scatter(1, sum_r)
            scatter(3, sum_i)
            yield
            for c, k, real, imag in planes_left(s):
                put_r(s, c, k, real, imag)
            start_right(s, G_CONJ)
            yield
            sum_r = jnp.zeros((WIN, WIN), jnp.float32)
            sum_i = jnp.zeros((WIN, WIN), jnp.float32)
            for c, k, real, imag in planes_right(s):
                m = 2 * c + k
                pr, pi = probe_ref[0, m], probe_ref[1, m]
                first_r, first_i = win[s, 0], win[s, 2]
                sum_r = sum_r + (pr * real + pi * imag)
                sum_i = sum_i + (pr * imag - pi * real)
                grad_r = first_r * real + first_i * imag
                grad_i = first_r * imag - first_i * real
                probe_grad_ref[0, m] = grad_r if s == 0 else probe_grad_ref[0, m] + grad_r
                probe_grad_ref[1, m] = grad_i if s == 0 else probe_grad_ref[1, m] + grad_i
            scatter(0, sum_r)
            scatter(2, sum_i)

        under_way = [steps(s) for s in scans]
        while under_way:
            under_way = [step for step in under_way if next(step, True) is None]

    pl.run_scoped(
        run, *[pltpu.ACC(c)((ROWS, 2 * WIN), jnp.float32) for _ in scans for c in chains for _ in range(BLOCKS)]
    )

    lane_all = lane_iota(ext_rows)
    east = jnp.zeros((ext_rows, LANES), jnp.float32)
    west = jnp.zeros((ext_rows, LANES), jnp.float32)
    for p in range(PLANES):
        for q in range(2):
            cols = slice(q * LANES, (q + 1) * LANES)
            north_rim_ref[p, :, cols] = grad[p, q, 0:HALO, :]
            center_ref[p, :, cols] = grad[p, q, HALO:last, :]
            south_rim_ref[p, :, cols] = grad[p, q, last:ext_rows, :]
        third = grad[p, 2]
        here = (lane_all >= p * HALO) & (lane_all < (p + 1) * HALO)
        east = jnp.where(here, turned(third, p * HALO), east)
        west = jnp.where(here, turned(third, (p - 3) * HALO), west)
    east_rim_ref[...] = east
    west_rim_ref[...] = west


def rim_corner_kernel(from_west_ref, from_east_ref, to_north_ref, to_south_ref):
    for k, ref in enumerate((from_west_ref, from_east_ref)):
        to_north_ref[k * HALO : (k + 1) * HALO, :] = ref[0:HALO, :]
        to_south_ref[k * HALO : (k + 1) * HALO, :] = ref[ref.shape[0] - HALO :, :]


def share_kernel(parts_ref, from_north_ref, from_south_ref, share_ref):
    del from_north_ref, from_south_ref
    share_ref[...] = jnp.broadcast_to(jnp.sum(parts_ref[...], axis=0)[None], share_ref.shape)


def object_kernel(
    center_ref, from_north_ref, from_south_ref, from_west_ref, from_east_ref, north_corners_ref, south_corners_ref,
    object_ref,
):
    rows = center_ref.shape[1]

    def rim(left, right, p):
        lane = lane_iota(left.shape[0])
        return (
            jnp.where(lane < HALO, turned(left, -p * HALO), 0.0),
            jnp.where(lane >= LANES - HALO, turned(right, (3 - p) * HALO), 0.0),
        )

    for p in range(PLANES):
        sides = rim(from_west_ref[HALO : HALO + rows, :], from_east_ref[HALO : HALO + rows, :], p)
        north = rim(north_corners_ref[0:HALO, :], north_corners_ref[HALO:, :], p)
        south = rim(south_corners_ref[0:HALO, :], south_corners_ref[HALO:, :], p)
        for q in range(2):
            cols = slice(q * LANES, (q + 1) * LANES)
            whole = center_ref[p, :, cols] + sides[q]
            object_ref[p, 0:HALO, cols] = whole[0:HALO] + from_north_ref[p, :, cols] + north[q]
            object_ref[p, HALO : rows - HALO, cols] = whole[HALO : rows - HALO]
            object_ref[p, rows - HALO :, cols] = whole[rows - HALO :] + from_south_ref[p, :, cols] + south[q]


def probe_kernel(total_ref, probe_ref, probe_new_ref):
    total = total_ref[...]
    squares = jnp.sum(total * total, axis=0, keepdims=True)
    mean = jnp.sum(squares, axis=1, keepdims=True) / (total.shape[0] * total.shape[1])
    probe_new_ref[...] = probe_ref[...] - total * (STEP_SIZE / jnp.sqrt(mean + EPSILON))


def vmem(count):
    return [pl.BlockSpec(memory_space=pltpu.VMEM)] * count


def f32(*shape):
    return jax.ShapeDtypeStruct(shape, jnp.float32)


def moved(block, axis, distance):
    count = lax.axis_size(axis)
    return lax.ppermute(block, axis, [(i, (i + distance) % count) for i in range(count)])


def cost(us):
    return pl.CostEstimate(flops=int(us * 1e9), bytes_accessed=int(us * 3e6), transcendentals=0)


def call(kernel, outs, ins, scratch=(), scalars=0, limit=2, us=0):
    return pl.pallas_call(
        kernel,
        out_shape=outs,
        in_specs=[pl.BlockSpec(memory_space=pltpu.SMEM)] * scalars + vmem(ins),
        out_specs=vmem(len(outs)) if isinstance(outs, list) else vmem(1)[0],
        scratch_shapes=scratch,
        compiler_params=pltpu.CompilerParams(vmem_limit_bytes=limit * 2**20),
        cost_estimate=cost(us) if us else None,
    )


def main_call(scans, rows, cols):
    ext_rows = rows + 2 * HALO
    pair = pltpu.VMEM((scans, MODES // 2, 2 * WIN, 2 * WIN), jnp.bfloat16)
    modes = pltpu.VMEM((scans, 2, MODES, WIN, WIN), jnp.float32)
    outs = [f32(2, MODES, WIN, WIN), f32(PLANES, rows, cols)]
    outs += [f32(PLANES, HALO, cols)] * 2 + [f32(ext_rows, LANES)] * 2 + [f32(PLANES, 3, ext_rows, LANES)]
    run = pl.pallas_call(
        main_kernel,
        out_shape=outs,
        in_specs=[pl.BlockSpec(memory_space=pltpu.SMEM)] + vmem(8),
        out_specs=vmem(len(outs)),
        scratch_shapes=[
            pair, pair, pair, pair, modes, modes,
            pltpu.VMEM((scans, PLANES, WIN, WIN), jnp.float32),
            pltpu.VMEM((scans, WIN, WIN), jnp.float32),
            pltpu.VMEM((PLANES, 3, ext_rows, LANES), jnp.float32),
        ],
        input_output_aliases={1: 6},
        compiler_params=pltpu.CompilerParams(vmem_limit_bytes=24 * 2**20),
        cost_estimate=cost(12),
    )
    return lambda *args: run(*args)[:6]


def on_device(object_tiles, probe_modes, offsets, amplitude):
    rows, cols = object_tiles.shape[2:]
    ext_rows = rows + 2 * HALO
    scans = offsets.shape[2]
    tile = object_tiles.reshape(PLANES, rows, cols)
    offset_pairs = jnp.swapaxes(offsets, 2, 3).reshape(2, scans)
    amp = amplitude.reshape(scans, WIN, WIN)
    flat = (2 * MODES * WIN, WIN)
    mats = jnp.asarray(matrices())
    devices = lax.axis_size("row") * lax.axis_size("col")

    north = moved(tile[:, rows - HALO :], "row", 1)
    south = moved(tile[:, :HALO], "row", -1)
    east_send, west_send = call(pack_kernel, [f32(rows, LANES)] * 2, 1)(tile)
    from_west = moved(east_send, "col", 1)
    from_east = moved(west_send, "col", -1)
    east_send, west_send = call(corner_kernel, [f32(2 * HALO, LANES)] * 2, 2)(north, south)
    west_corners = moved(east_send, "col", 1)
    east_corners = moved(west_send, "col", -1)

    ext = call(assemble_kernel, f32(PLANES, 3, ext_rows, LANES), 3, us=4)(tile, north, south)
    probe_grad, center, north_rim, south_rim, east_rim, west_rim = main_call(scans, rows, cols)(
        offset_pairs, ext, from_west, from_east, west_corners, east_corners, amp, probe_modes, mats
    )

    parts = lax.all_to_all(probe_grad.reshape(devices, -1, LANES), BOTH, 0, 0, tiled=True)
    rim_from_west = moved(east_rim, "col", 1)
    rim_from_east = moved(west_rim, "col", -1)
    from_south = moved(north_rim, "row", -1)
    from_north = moved(south_rim, "row", 1)
    share = call(share_kernel, f32(*parts.shape), 3)(parts, from_north, from_south)
    total = lax.all_to_all(share, BOTH, 0, 0, tiled=True)
    to_north, to_south = call(rim_corner_kernel, [f32(2 * HALO, LANES)] * 2, 2)(rim_from_west, rim_from_east)
    south_corners = moved(to_north, "row", -1)
    north_corners = moved(to_south, "row", 1)
    object_grad = call(object_kernel, f32(PLANES, rows, cols), 7)(
        center, from_north, from_south, rim_from_west, rim_from_east, north_corners, south_corners
    )
    probe_new = call(probe_kernel, f32(*flat), 2)(total.reshape(flat), probe_modes.reshape(flat))
    return object_grad.reshape(object_tiles.shape), probe_new.reshape(probe_modes.shape)


def solution(mesh):
    placed = (
        P(None, None, "row", "col"),
        P(),
        P("row", "col", None, None),
        P("row", "col", None, None, None),
    )
    return jax.shard_map(
        on_device,
        mesh=mesh,
        in_specs=placed,
        out_specs=(P(None, None, "row", "col"), P()),
        check_vma=False,
    )
```

```python
import jax
import jax.numpy as jnp
import numpy as np
from jax import lax
from jax.experimental import pallas as pl
from jax.experimental.pallas import tpu as pltpu
from jax.sharding import PartitionSpec as P

HALO = 32
WIN = 128
MODES = 4
PLANES = 4
LANES = 128
PROP = 0.002
SHIFT_AMP = 0.5
STEP_SIZE = 0.5
EPSILON = 1e-06
BOTH = ("row", "col")


def matrices():
    k = np.arange(WIN)
    c = np.exp(-2j * np.pi * (np.outer(k, k) % WIN) / WIN) / np.sqrt(WIN)
    f = ((k + WIN // 2) % WIN - WIN // 2).astype(np.float64)
    g = c.conj() @ np.diag(np.exp(-1j * PROP * f * f)) @ c
    stack = []
    for m in (c, c.conj(), g, g.conj()):
        w = np.block([[m.real, m.imag], [-m.imag, m.real]]).astype(np.float32)
        high = w.astype(jnp.bfloat16)
        low = (w - high.astype(np.float32)).astype(jnp.bfloat16)
        stack.append(np.stack([high, low]))
    return np.stack(stack)


C, C_CONJ, G, G_CONJ = range(4)
BLOCKS = 2
ROWS = 2 * WIN // BLOCKS


def lane_iota(rows):
    return lax.broadcasted_iota(jnp.int32, (rows, LANES), 1)


def edges(src, rows):
    lane = lane_iota(rows)
    east = jnp.zeros((rows, LANES), jnp.float32)
    west = jnp.zeros((rows, LANES), jnp.float32)
    for p in range(PLANES):
        here = (lane >= p * HALO) & (lane < (p + 1) * HALO)
        east = jnp.where(here, turned(src[p, :, LANES : 2 * LANES], (p - 3) * HALO), east)
        west = jnp.where(here, turned(src[p, :, 0:LANES], p * HALO), west)
    return east, west


def turned(block, shift):
    return pltpu.roll(block, shift % LANES, 1) if shift % LANES else block


def pack_kernel(tile_ref, east_ref, west_ref):
    east_ref[...], west_ref[...] = edges(tile_ref, tile_ref.shape[1])


def corner_kernel(north_ref, south_ref, east_ref, west_ref):
    east_ref[0:HALO, :], west_ref[0:HALO, :] = edges(north_ref, HALO)
    east_ref[HALO:, :], west_ref[HALO:, :] = edges(south_ref, HALO)


def split(value):
    high = value.astype(jnp.bfloat16)
    return high, (value - high.astype(jnp.float32)).astype(jnp.bfloat16)


def dot(left, right):
    return jnp.dot(left, right, preferred_element_type=jnp.float32)


def assemble_kernel(tile_ref, north_ref, south_ref, ext):
    rows = tile_ref.shape[1]
    for p in range(PLANES):
        for q in range(2):
            cols = slice(q * LANES, (q + 1) * LANES)
            ext[p, q, 0:HALO, :] = north_ref[p, :, cols]
            ext[p, q, HALO : HALO + rows, :] = tile_ref[p, :, cols]
            ext[p, q, HALO + rows :, :] = south_ref[p, :, cols]


def place(offsets_ref, s, q_count=3):
    start = lax.rem(offsets_ref[1, s] + (q_count * LANES - HALO), q_count * LANES)
    first = lax.div(start, LANES)
    return offsets_ref[0, s], first, lax.rem(first + 1, q_count), lax.rem(start, LANES)


def main_kernel(
    offsets_ref, ext_in, from_west_ref, from_east_ref, west_corners_ref, east_corners_ref, amp_ref, probe_ref, mat_ref,
    probe_grad_ref, center_ref, north_rim_ref, south_rim_ref, east_rim_ref, west_rim_ref, ext,
    rh, rl, lh, ll, field, d_keep, win, factor, grad,
):
    del ext_in
    ext_rows = ext.shape[2]
    last = ext_rows - HALO

    def beside(left, right, p):
        low = lane_iota(left.shape[0]) < 2 * HALO
        return jnp.where(low, turned(right, -p * HALO), turned(left, (3 - p) * HALO))

    for p in range(PLANES):
        ext[p, 2, 0:HALO, :] = beside(west_corners_ref[0:HALO, :], east_corners_ref[0:HALO, :], p)
        ext[p, 2, HALO:last, :] = beside(from_west_ref[...], from_east_ref[...], p)
        ext[p, 2, last:ext_rows, :] = beside(west_corners_ref[HALO:, :], east_corners_ref[HALO:, :], p)

    lane = lane_iota(WIN)
    chains = range(MODES // 2)
    scans = range(amp_ref.shape[0])

    def put(high, low, at, value):
        high[at], low[at] = split(value)

    def run(*accs):
        def blocks(s, c):
            first = (s * len(chains) + c) * BLOCKS
            return accs[first : first + BLOCKS]

        def multiply(s, c, rhs, lhss, stage):
            pltpu.matmul_push_rhs(rhs, stage, c)
            for lhs in lhss:
                for b, acc in enumerate(blocks(s, c)):
                    pltpu.matmul_acc_lhs(acc, lhs[b * ROWS : (b + 1) * ROWS, :], stage)
                    stage = None

        def start_right(s, which):
            for c in chains:
                multiply(s, c, mat_ref[which, 0], (rh[s, c], rl[s, c]), 0)
                multiply(s, c, mat_ref[which, 1], (rh[s, c],), 1)

        def start_left(s, which):
            high, low = mat_ref[which ^ 1, 0], mat_ref[which ^ 1, 1]
            for c in chains:
                multiply(s, c, lh[s, c], (high, low), 0)
                multiply(s, c, ll[s, c], (high,), 1)

        def planes_right(s):
            for c in chains:
                out = jnp.concatenate([pltpu.matmul_pop(acc) for acc in blocks(s, c)], axis=0)
                for k in range(2):
                    yield c, k, out[k * WIN : (k + 1) * WIN, 0:WIN], out[k * WIN : (k + 1) * WIN, WIN:]

        def planes_left(s):
            for c in chains:
                out = jnp.concatenate([pltpu.matmul_pop(acc) for acc in blocks(s, c)], axis=0)
                for k in range(2):
                    yield c, k, out[0:WIN, k * WIN : (k + 1) * WIN], out[WIN:, k * WIN : (k + 1) * WIN]

        def put_r(s, c, k, real, imag):
            rows = slice(k * WIN, (k + 1) * WIN)
            put(rh, rl, (s, c, rows, slice(0, WIN)), real)
            put(rh, rl, (s, c, rows, slice(WIN, 2 * WIN)), imag)

        def put_l(s, c, k, real, imag):
            cols = slice(k * WIN, (k + 1) * WIN)
            put(lh, ll, (s, c, slice(0, WIN), cols), real)
            put(lh, ll, (s, c, slice(WIN, 2 * WIN), cols), imag)

        def steps(s):
            row, q, q_next, shift = place(offsets_ref, s)
            back = lax.rem(LANES - shift, LANES)

            def scatter(p, value):
                value = pltpu.roll(value, shift, 1)
                grad[p, q, pl.ds(row, WIN), :] += jnp.where(lane >= shift, value, 0.0)
                grad[p, q_next, pl.ds(row, WIN), :] += jnp.where(lane < shift, value, 0.0)

            for p in range(PLANES):
                a = pltpu.roll(ext[p, q, pl.ds(row, WIN), :], back, 1)
                b = pltpu.roll(ext[p, q_next, pl.ds(row, WIN), :], back, 1)
                win[s, p] = jnp.where(lane < LANES - shift, a, b)
            for c in chains:
                for k in range(2):
                    pr, pi = probe_ref[0, 2 * c + k], probe_ref[1, 2 * c + k]
                    put_r(s, c, k, pr * win[s, 0] - pi * win[s, 2], pr * win[s, 2] + pi * win[s, 0])
            start_right(s, G)
            if s == 0:
                grad[...] = jnp.zeros_like(grad)
            yield
            for c, k, real, imag in planes_right(s):
                put_l(s, c, k, real, imag)
            start_left(s, G)
            yield
            for c, k, real, imag in planes_left(s):
                m = 2 * c + k
                d_keep[s, 0, m] = real
                d_keep[s, 1, m] = imag
                second_r, second_i = win[s, 1], win[s, 3]
                put_l(s, c, k, real * second_r - imag * second_i, real * second_i + imag * second_r)
            start_left(s, C)
            yield
            for c, k, real, imag in planes_left(s):
                put_r(s, c, k, real, imag)
            start_right(s, C)
            yield
            intensity = jnp.full((WIN, WIN), SHIFT_AMP, jnp.float32)
            for c, k, real, imag in planes_right(s):
                m = 2 * c + k
                field[s, 0, m] = real
                field[s, 1, m] = imag
                intensity = intensity + (real * real + imag * imag)
            factor[s] = 2.0 - 2.0 * amp_ref[s] / jnp.sqrt(intensity)
            for c in chains:
                for k in range(2):
                    m = 2 * c + k
                    put_r(s, c, k, field[s, 0, m] * factor[s], field[s, 1, m] * factor[s])
            start_right(s, C_CONJ)
            yield
            for c, k, real, imag in planes_right(s):
                put_l(s, c, k, real, imag)
            start_left(s, C_CONJ)
            yield
            sum_r = jnp.zeros((WIN, WIN), jnp.float32)
            sum_i = jnp.zeros((WIN, WIN), jnp.float32)
            for c, k, real, imag in planes_left(s):
                dr, di = d_keep[s, 0, 2 * c + k], d_keep[s, 1, 2 * c + k]
                second_r, second_i = win[s, 1], win[s, 3]
                sum_r = sum_r + (dr * real + di * imag)
                sum_i = sum_i + (dr * imag - di * real)
                put_l(s, c, k, second_r * real + second_i * imag, second_r * imag - second_i * real)
            start_left(s, G_CONJ)
            scatter(1, sum_r)
            scatter(3, sum_i)
            yield
            for c, k, real, imag in planes_left(s):
                put_r(s, c, k, real, imag)
            start_right(s, G_CONJ)
            yield
            sum_r = jnp.zeros((WIN, WIN), jnp.float32)
            sum_i = jnp.zeros((WIN, WIN), jnp.float32)
            for c, k, real, imag in planes_right(s):
                m = 2 * c + k
                pr, pi = probe_ref[0, m], probe_ref[1, m]
                first_r, first_i = win[s, 0], win[s, 2]
                sum_r = sum_r + (pr * real + pi * imag)
                sum_i = sum_i + (pr * imag - pi * real)
                grad_r = first_r * real + first_i * imag
                grad_i = first_r * imag - first_i * real
                probe_grad_ref[0, m] = grad_r if s == 0 else probe_grad_ref[0, m] + grad_r
                probe_grad_ref[1, m] = grad_i if s == 0 else probe_grad_ref[1, m] + grad_i
            scatter(0, sum_r)
            scatter(2, sum_i)

        under_way = [steps(s) for s in scans]
        while under_way:
            under_way = [step for step in under_way if next(step, True) is None]

    pl.run_scoped(
        run, *[pltpu.ACC(c)((ROWS, 2 * WIN), jnp.float32) for _ in scans for c in chains for _ in range(BLOCKS)]
    )

    lane_all = lane_iota(ext_rows)
    east = jnp.zeros((ext_rows, LANES), jnp.float32)
    west = jnp.zeros((ext_rows, LANES), jnp.float32)
    for p in range(PLANES):
        for q in range(2):
            cols = slice(q * LANES, (q + 1) * LANES)
            north_rim_ref[p, :, cols] = grad[p, q, 0:HALO, :]
            center_ref[p, :, cols] = grad[p, q, HALO:last, :]
            south_rim_ref[p, :, cols] = grad[p, q, last:ext_rows, :]
        third = grad[p, 2]
        here = (lane_all >= p * HALO) & (lane_all < (p + 1) * HALO)
        east = jnp.where(here, turned(third, p * HALO), east)
        west = jnp.where(here, turned(third, (p - 3) * HALO), west)
    east_rim_ref[...] = east
    west_rim_ref[...] = west


def rim_corner_kernel(from_west_ref, from_east_ref, to_north_ref, to_south_ref):
    for k, ref in enumerate((from_west_ref, from_east_ref)):
        to_north_ref[k * HALO : (k + 1) * HALO, :] = ref[0:HALO, :]
        to_south_ref[k * HALO : (k + 1) * HALO, :] = ref[ref.shape[0] - HALO :, :]


def share_kernel(parts_ref, *refs):
    share_ref = refs[-1]
    share_ref[...] = jnp.broadcast_to(jnp.sum(parts_ref[...], axis=0)[None], share_ref.shape)


def object_kernel(
    center_ref, from_north_ref, from_south_ref, from_west_ref, from_east_ref, north_corners_ref, south_corners_ref,
    object_ref,
):
    rows = center_ref.shape[1]

    def rim(left, right, p):
        lane = lane_iota(left.shape[0])
        return (
            jnp.where(lane < HALO, turned(left, -p * HALO), 0.0),
            jnp.where(lane >= LANES - HALO, turned(right, (3 - p) * HALO), 0.0),
        )

    for p in range(PLANES):
        sides = rim(from_west_ref[HALO : HALO + rows, :], from_east_ref[HALO : HALO + rows, :], p)
        north = rim(north_corners_ref[0:HALO, :], north_corners_ref[HALO:, :], p)
        south = rim(south_corners_ref[0:HALO, :], south_corners_ref[HALO:, :], p)
        for q in range(2):
            cols = slice(q * LANES, (q + 1) * LANES)
            whole = center_ref[p, :, cols] + sides[q]
            object_ref[p, 0:HALO, cols] = whole[0:HALO] + from_north_ref[p, :, cols] + north[q]
            object_ref[p, HALO : rows - HALO, cols] = whole[HALO : rows - HALO]
            object_ref[p, rows - HALO :, cols] = whole[rows - HALO :] + from_south_ref[p, :, cols] + south[q]


def probe_kernel(total_ref, probe_ref, probe_new_ref):
    total = total_ref[...]
    squares = jnp.sum(total * total, axis=0, keepdims=True)
    mean = jnp.sum(squares, axis=1, keepdims=True) / (total.shape[0] * total.shape[1])
    probe_new_ref[...] = probe_ref[...] - total * (STEP_SIZE / jnp.sqrt(mean + EPSILON))


def vmem(count):
    return [pl.BlockSpec(memory_space=pltpu.VMEM)] * count


def f32(*shape):
    return jax.ShapeDtypeStruct(shape, jnp.float32)


def moved(block, axis, distance):
    count = lax.axis_size(axis)
    return lax.ppermute(block, axis, [(i, (i + distance) % count) for i in range(count)])


def cost(us):
    return pl.CostEstimate(flops=int(us * 1e9), bytes_accessed=int(us * 3e6), transcendentals=0)


def call(kernel, outs, ins, scratch=(), scalars=0, limit=2, us=0):
    return pl.pallas_call(
        kernel,
        out_shape=outs,
        in_specs=[pl.BlockSpec(memory_space=pltpu.SMEM)] * scalars + vmem(ins),
        out_specs=vmem(len(outs)) if isinstance(outs, list) else vmem(1)[0],
        scratch_shapes=scratch,
        compiler_params=pltpu.CompilerParams(vmem_limit_bytes=limit * 2**20),
        cost_estimate=cost(us) if us else None,
    )


def main_call(scans, rows, cols):
    ext_rows = rows + 2 * HALO
    pair = pltpu.VMEM((scans, MODES // 2, 2 * WIN, 2 * WIN), jnp.bfloat16)
    modes = pltpu.VMEM((scans, 2, MODES, WIN, WIN), jnp.float32)
    outs = [f32(2, MODES, WIN, WIN), f32(PLANES, rows, cols)]
    outs += [f32(PLANES, HALO, cols)] * 2 + [f32(ext_rows, LANES)] * 2 + [f32(PLANES, 3, ext_rows, LANES)]
    run = pl.pallas_call(
        main_kernel,
        out_shape=outs,
        in_specs=[pl.BlockSpec(memory_space=pltpu.SMEM)] + vmem(8),
        out_specs=vmem(len(outs)),
        scratch_shapes=[
            pair, pair, pair, pair, modes, modes,
            pltpu.VMEM((scans, PLANES, WIN, WIN), jnp.float32),
            pltpu.VMEM((scans, WIN, WIN), jnp.float32),
            pltpu.VMEM((PLANES, 3, ext_rows, LANES), jnp.float32),
        ],
        input_output_aliases={1: 6},
        compiler_params=pltpu.CompilerParams(vmem_limit_bytes=24 * 2**20),
        cost_estimate=cost(12),
    )
    return lambda *args: run(*args)[:6]


def on_device(object_tiles, probe_modes, offsets, amplitude):
    rows, cols = object_tiles.shape[2:]
    ext_rows = rows + 2 * HALO
    scans = offsets.shape[2]
    tile = object_tiles.reshape(PLANES, rows, cols)
    offset_pairs = jnp.swapaxes(offsets, 2, 3).reshape(2, scans)
    amp = amplitude.reshape(scans, WIN, WIN)
    flat = (2 * MODES * WIN, WIN)
    mats = jnp.asarray(matrices())
    devices = lax.axis_size("row") * lax.axis_size("col")

    north = moved(tile[:, rows - HALO :], "row", 1)
    south = moved(tile[:, :HALO], "row", -1)
    east_send, west_send = call(pack_kernel, [f32(rows, LANES)] * 2, 1, us=1)(tile)
    from_west = moved(east_send, "col", 1)
    from_east = moved(west_send, "col", -1)
    east_send, west_send = call(corner_kernel, [f32(2 * HALO, LANES)] * 2, 2, us=1)(north, south)
    west_corners = moved(east_send, "col", 1)
    east_corners = moved(west_send, "col", -1)

    ext = call(assemble_kernel, f32(PLANES, 3, ext_rows, LANES), 3, us=4)(tile, north, south)
    probe_grad, center, north_rim, south_rim, east_rim, west_rim = main_call(scans, rows, cols)(
        offset_pairs, ext, from_west, from_east, west_corners, east_corners, amp, probe_modes, mats
    )

    parts = lax.all_to_all(probe_grad.reshape(devices, -1, LANES), BOTH, 0, 0, tiled=True)
    rim_from_west = moved(east_rim, "col", 1)
    rim_from_east = moved(west_rim, "col", -1)
    from_south = moved(north_rim, "row", -1)
    from_north = moved(south_rim, "row", 1)
    share = call(share_kernel, f32(*parts.shape), 5)(
        parts, rim_from_west, rim_from_east, from_north, from_south
    )
    total = lax.all_to_all(share, BOTH, 0, 0, tiled=True)
    to_north, to_south = call(rim_corner_kernel, [f32(2 * HALO, LANES)] * 2, 2)(rim_from_west, rim_from_east)
    south_corners = moved(to_north, "row", -1)
    north_corners = moved(to_south, "row", 1)
    object_grad = call(object_kernel, f32(PLANES, rows, cols), 7)(
        center, from_north, from_south, rim_from_west, rim_from_east, north_corners, south_corners
    )
    probe_new = call(probe_kernel, f32(*flat), 2)(total.reshape(flat), probe_modes.reshape(flat))
    return object_grad.reshape(object_tiles.shape), probe_new.reshape(probe_modes.shape)


def solution(mesh):
    placed = (
        P(None, None, "row", "col"),
        P(),
        P("row", "col", None, None),
        P("row", "col", None, None, None),
    )
    return jax.shard_map(
        on_device,
        mesh=mesh,
        in_specs=placed,
        out_specs=(P(None, None, "row", "col"), P()),
        check_vma=False,
    )
```

```python
import jax
import jax.numpy as jnp
import numpy as np
from jax import lax
from jax.experimental import pallas as pl
from jax.experimental.pallas import tpu as pltpu
from jax.sharding import PartitionSpec as P

HALO = 32
WIN = 128
MODES = 4
PLANES = 4
LANES = 128
PROP = 0.002
SHIFT_AMP = 0.5
STEP_SIZE = 0.5
EPSILON = 1e-06
BOTH = ("row", "col")


def matrices():
    k = np.arange(WIN)
    c = np.exp(-2j * np.pi * (np.outer(k, k) % WIN) / WIN) / np.sqrt(WIN)
    f = ((k + WIN // 2) % WIN - WIN // 2).astype(np.float64)
    g = c.conj() @ np.diag(np.exp(-1j * PROP * f * f)) @ c
    stack = []
    for m in (c, c.conj(), g, g.conj()):
        w = np.block([[m.real, m.imag], [-m.imag, m.real]]).astype(np.float32)
        high = w.astype(jnp.bfloat16)
        low = (w - high.astype(np.float32)).astype(jnp.bfloat16)
        stack.append(np.stack([high, low]))
    return np.stack(stack)


C, C_CONJ, G, G_CONJ = range(4)
BLOCKS = 2
ROWS = 2 * WIN // BLOCKS


def lane_iota(rows):
    return lax.broadcasted_iota(jnp.int32, (rows, LANES), 1)


def edges(src, rows):
    lane = lane_iota(rows)
    east = jnp.zeros((rows, LANES), jnp.float32)
    west = jnp.zeros((rows, LANES), jnp.float32)
    for p in range(PLANES):
        here = (lane >= p * HALO) & (lane < (p + 1) * HALO)
        east = jnp.where(here, turned(src[p, :, LANES : 2 * LANES], (p - 3) * HALO), east)
        west = jnp.where(here, turned(src[p, :, 0:LANES], p * HALO), west)
    return east, west


def turned(block, shift):
    return pltpu.roll(block, shift % LANES, 1) if shift % LANES else block


def pack_kernel(tile_ref, east_ref, west_ref):
    east_ref[...], west_ref[...] = edges(tile_ref, tile_ref.shape[1])


def corner_kernel(north_ref, south_ref, east_ref, west_ref):
    east_ref[0:HALO, :], west_ref[0:HALO, :] = edges(north_ref, HALO)
    east_ref[HALO:, :], west_ref[HALO:, :] = edges(south_ref, HALO)


def split(value):
    high = value.astype(jnp.bfloat16)
    return high, (value - high.astype(jnp.float32)).astype(jnp.bfloat16)


def dot(left, right):
    return jnp.dot(left, right, preferred_element_type=jnp.float32)


def assemble_kernel(tile_ref, north_ref, south_ref, ext):
    rows = tile_ref.shape[1]
    for p in range(PLANES):
        for q in range(2):
            cols = slice(q * LANES, (q + 1) * LANES)
            ext[p, q, 0:HALO, :] = north_ref[p, :, cols]
            ext[p, q, HALO : HALO + rows, :] = tile_ref[p, :, cols]
            ext[p, q, HALO + rows :, :] = south_ref[p, :, cols]


def place(offsets_ref, s, q_count=3):
    start = lax.rem(offsets_ref[1, s] + (q_count * LANES - HALO), q_count * LANES)
    first = lax.div(start, LANES)
    return offsets_ref[0, s], first, lax.rem(first + 1, q_count), lax.rem(start, LANES)


def main_kernel(
    offsets_ref, ext_in, from_west_ref, from_east_ref, west_corners_ref, east_corners_ref, amp_ref, probe_ref, mat_ref,
    probe_grad_ref, center_ref, north_rim_ref, south_rim_ref, east_rim_ref, west_rim_ref, ext,
    rh, rl, lh, ll, field, d_keep, win, factor, grad,
):
    del ext_in
    ext_rows = ext.shape[2]
    last = ext_rows - HALO

    def beside(left, right, p):
        low = lane_iota(left.shape[0]) < 2 * HALO
        return jnp.where(low, turned(right, -p * HALO), turned(left, (3 - p) * HALO))

    for p in range(PLANES):
        ext[p, 2, 0:HALO, :] = beside(west_corners_ref[0:HALO, :], east_corners_ref[0:HALO, :], p)
        ext[p, 2, HALO:last, :] = beside(from_west_ref[...], from_east_ref[...], p)
        ext[p, 2, last:ext_rows, :] = beside(west_corners_ref[HALO:, :], east_corners_ref[HALO:, :], p)

    lane = lane_iota(WIN)
    chains = range(MODES // 2)
    scans = range(amp_ref.shape[0])

    def put(high, low, at, value):
        high[at], low[at] = split(value)

    def run(*accs):
        def blocks(s, c):
            first = (s * len(chains) + c) * BLOCKS
            return accs[first : first + BLOCKS]

        def multiply(s, c, rhs, lhss, stage):
            pltpu.matmul_push_rhs(rhs, stage, c)
            for lhs in lhss:
                for b, acc in enumerate(blocks(s, c)):
                    pltpu.matmul_acc_lhs(acc, lhs[b * ROWS : (b + 1) * ROWS, :], stage)
                    stage = None

        def start_right(s, which):
            for c in chains:
                multiply(s, c, mat_ref[which, 0], (rh[s, c], rl[s, c]), 0)
                multiply(s, c, mat_ref[which, 1], (rh[s, c],), 1)

        def start_left(s, which):
            high, low = mat_ref[which ^ 1, 0], mat_ref[which ^ 1, 1]
            for c in chains:
                multiply(s, c, lh[s, c], (high, low), 0)
                multiply(s, c, ll[s, c], (high,), 1)

        def planes_right(s):
            for c in chains:
                out = jnp.concatenate([pltpu.matmul_pop(acc) for acc in blocks(s, c)], axis=0)
                for k in range(2):
                    yield c, k, out[k * WIN : (k + 1) * WIN, 0:WIN], out[k * WIN : (k + 1) * WIN, WIN:]

        def planes_left(s):
            for c in chains:
                out = jnp.concatenate([pltpu.matmul_pop(acc) for acc in blocks(s, c)], axis=0)
                for k in range(2):
                    yield c, k, out[0:WIN, k * WIN : (k + 1) * WIN], out[WIN:, k * WIN : (k + 1) * WIN]

        def put_r(s, c, k, real, imag):
            rows = slice(k * WIN, (k + 1) * WIN)
            put(rh, rl, (s, c, rows, slice(0, WIN)), real)
            put(rh, rl, (s, c, rows, slice(WIN, 2 * WIN)), imag)

        def put_l(s, c, k, real, imag):
            cols = slice(k * WIN, (k + 1) * WIN)
            put(lh, ll, (s, c, slice(0, WIN), cols), real)
            put(lh, ll, (s, c, slice(WIN, 2 * WIN), cols), imag)

        def steps(s):
            row, q, q_next, shift = place(offsets_ref, s)
            back = lax.rem(LANES - shift, LANES)

            def scatter(p, value):
                value = pltpu.roll(value, shift, 1)
                grad[p, q, pl.ds(row, WIN), :] += jnp.where(lane >= shift, value, 0.0)
                grad[p, q_next, pl.ds(row, WIN), :] += jnp.where(lane < shift, value, 0.0)

            for p in range(PLANES):
                a = pltpu.roll(ext[p, q, pl.ds(row, WIN), :], back, 1)
                b = pltpu.roll(ext[p, q_next, pl.ds(row, WIN), :], back, 1)
                win[s, p] = jnp.where(lane < LANES - shift, a, b)
            for c in chains:
                for k in range(2):
                    pr, pi = probe_ref[0, 2 * c + k], probe_ref[1, 2 * c + k]
                    put_r(s, c, k, pr * win[s, 0] - pi * win[s, 2], pr * win[s, 2] + pi * win[s, 0])
            start_right(s, G)
            if s == 0:
                grad[...] = jnp.zeros_like(grad)
            yield
            for c, k, real, imag in planes_right(s):
                put_l(s, c, k, real, imag)
            start_left(s, G)
            yield
            for c, k, real, imag in planes_left(s):
                m = 2 * c + k
                d_keep[s, 0, m] = real
                d_keep[s, 1, m] = imag
                second_r, second_i = win[s, 1], win[s, 3]
                put_l(s, c, k, real * second_r - imag * second_i, real * second_i + imag * second_r)
            start_left(s, C)
            yield
            for c, k, real, imag in planes_left(s):
                put_r(s, c, k, real, imag)
            start_right(s, C)
            yield
            intensity = jnp.full((WIN, WIN), SHIFT_AMP, jnp.float32)
            for c, k, real, imag in planes_right(s):
                m = 2 * c + k
                field[s, 0, m] = real
                field[s, 1, m] = imag
                intensity = intensity + (real * real + imag * imag)
            factor[s] = 2.0 - 2.0 * amp_ref[s] / jnp.sqrt(intensity)
            for c in chains:
                for k in range(2):
                    m = 2 * c + k
                    put_r(s, c, k, field[s, 0, m] * factor[s], field[s, 1, m] * factor[s])
            start_right(s, C_CONJ)
            yield
            for c, k, real, imag in planes_right(s):
                put_l(s, c, k, real, imag)
            start_left(s, C_CONJ)
            yield
            sum_r = jnp.zeros((WIN, WIN), jnp.float32)
            sum_i = jnp.zeros((WIN, WIN), jnp.float32)
            for c, k, real, imag in planes_left(s):
                dr, di = d_keep[s, 0, 2 * c + k], d_keep[s, 1, 2 * c + k]
                second_r, second_i = win[s, 1], win[s, 3]
                sum_r = sum_r + (dr * real + di * imag)
                sum_i = sum_i + (dr * imag - di * real)
                put_l(s, c, k, second_r * real + second_i * imag, second_r * imag - second_i * real)
            start_left(s, G_CONJ)
            scatter(1, sum_r)
            scatter(3, sum_i)
            yield
            for c, k, real, imag in planes_left(s):
                put_r(s, c, k, real, imag)
            start_right(s, G_CONJ)
            yield
            sum_r = jnp.zeros((WIN, WIN), jnp.float32)
            sum_i = jnp.zeros((WIN, WIN), jnp.float32)
            for c, k, real, imag in planes_right(s):
                m = 2 * c + k
                pr, pi = probe_ref[0, m], probe_ref[1, m]
                first_r, first_i = win[s, 0], win[s, 2]
                sum_r = sum_r + (pr * real + pi * imag)
                sum_i = sum_i + (pr * imag - pi * real)
                grad_r = first_r * real + first_i * imag
                grad_i = first_r * imag - first_i * real
                probe_grad_ref[0, m] = grad_r if s == 0 else probe_grad_ref[0, m] + grad_r
                probe_grad_ref[1, m] = grad_i if s == 0 else probe_grad_ref[1, m] + grad_i
            scatter(0, sum_r)
            scatter(2, sum_i)

        under_way = [steps(s) for s in scans]
        while under_way:
            under_way = [step for step in under_way if next(step, True) is None]

    pl.run_scoped(
        run, *[pltpu.ACC(c)((ROWS, 2 * WIN), jnp.float32) for _ in scans for c in chains for _ in range(BLOCKS)]
    )

    lane_all = lane_iota(ext_rows)
    east = jnp.zeros((ext_rows, LANES), jnp.float32)
    west = jnp.zeros((ext_rows, LANES), jnp.float32)
    for p in range(PLANES):
        for q in range(2):
            cols = slice(q * LANES, (q + 1) * LANES)
            north_rim_ref[p, :, cols] = grad[p, q, 0:HALO, :]
            center_ref[p, :, cols] = grad[p, q, HALO:last, :]
            south_rim_ref[p, :, cols] = grad[p, q, last:ext_rows, :]
        third = grad[p, 2]
        here = (lane_all >= p * HALO) & (lane_all < (p + 1) * HALO)
        east = jnp.where(here, turned(third, p * HALO), east)
        west = jnp.where(here, turned(third, (p - 3) * HALO), west)
    east_rim_ref[...] = east
    west_rim_ref[...] = west


def rim_corner_kernel(from_west_ref, from_east_ref, to_north_ref, to_south_ref):
    for k, ref in enumerate((from_west_ref, from_east_ref)):
        to_north_ref[k * HALO : (k + 1) * HALO, :] = ref[0:HALO, :]
        to_south_ref[k * HALO : (k + 1) * HALO, :] = ref[ref.shape[0] - HALO :, :]


def share_kernel(parts_ref, *refs):
    share_ref = refs[-1]
    share_ref[...] = jnp.broadcast_to(jnp.sum(parts_ref[...], axis=0)[None], share_ref.shape)


def object_kernel(
    center_ref, from_north_ref, from_south_ref, from_west_ref, from_east_ref, north_corners_ref, south_corners_ref,
    object_ref,
):
    rows = center_ref.shape[1]

    def rim(left, right, p):
        lane = lane_iota(left.shape[0])
        return (
            jnp.where(lane < HALO, turned(left, -p * HALO), 0.0),
            jnp.where(lane >= LANES - HALO, turned(right, (3 - p) * HALO), 0.0),
        )

    for p in range(PLANES):
        sides = rim(from_west_ref[HALO : HALO + rows, :], from_east_ref[HALO : HALO + rows, :], p)
        north = rim(north_corners_ref[0:HALO, :], north_corners_ref[HALO:, :], p)
        south = rim(south_corners_ref[0:HALO, :], south_corners_ref[HALO:, :], p)
        for q in range(2):
            cols = slice(q * LANES, (q + 1) * LANES)
            whole = center_ref[p, :, cols] + sides[q]
            object_ref[p, 0:HALO, cols] = whole[0:HALO] + from_north_ref[p, :, cols] + north[q]
            object_ref[p, HALO : rows - HALO, cols] = whole[HALO : rows - HALO]
            object_ref[p, rows - HALO :, cols] = whole[rows - HALO :] + from_south_ref[p, :, cols] + south[q]


def probe_kernel(total_ref, probe_ref, probe_new_ref):
    total = total_ref[...]
    squares = jnp.sum(total * total, axis=0, keepdims=True)
    mean = jnp.sum(squares, axis=1, keepdims=True) / (total.shape[0] * total.shape[1])
    probe_new_ref[...] = probe_ref[...] - total * (STEP_SIZE / jnp.sqrt(mean + EPSILON))


def vmem(count):
    return [pl.BlockSpec(memory_space=pltpu.VMEM)] * count


def f32(*shape):
    return jax.ShapeDtypeStruct(shape, jnp.float32)


def moved(block, axis, distance):
    count = lax.axis_size(axis)
    return lax.ppermute(block, axis, [(i, (i + distance) % count) for i in range(count)])


def cost(us):
    return pl.CostEstimate(flops=int(us * 1e9), bytes_accessed=int(us * 3e6), transcendentals=0)


def call(kernel, outs, ins, scratch=(), scalars=0, limit=2, us=0):
    return pl.pallas_call(
        kernel,
        out_shape=outs,
        in_specs=[pl.BlockSpec(memory_space=pltpu.SMEM)] * scalars + vmem(ins),
        out_specs=vmem(len(outs)) if isinstance(outs, list) else vmem(1)[0],
        scratch_shapes=scratch,
        compiler_params=pltpu.CompilerParams(vmem_limit_bytes=limit * 2**20),
        cost_estimate=cost(us) if us else None,
    )


def main_call(scans, rows, cols):
    ext_rows = rows + 2 * HALO
    pair = pltpu.VMEM((scans, MODES // 2, 2 * WIN, 2 * WIN), jnp.bfloat16)
    modes = pltpu.VMEM((scans, 2, MODES, WIN, WIN), jnp.float32)
    outs = [f32(2, MODES, WIN, WIN), f32(PLANES, rows, cols)]
    outs += [f32(PLANES, HALO, cols)] * 2 + [f32(ext_rows, LANES)] * 2 + [f32(PLANES, 3, ext_rows, LANES)]
    run = pl.pallas_call(
        main_kernel,
        out_shape=outs,
        in_specs=[pl.BlockSpec(memory_space=pltpu.SMEM)] + vmem(8),
        out_specs=vmem(len(outs)),
        scratch_shapes=[
            pair, pair, pair, pair, modes, modes,
            pltpu.VMEM((scans, PLANES, WIN, WIN), jnp.float32),
            pltpu.VMEM((scans, WIN, WIN), jnp.float32),
            pltpu.VMEM((PLANES, 3, ext_rows, LANES), jnp.float32),
        ],
        input_output_aliases={1: 6},
        compiler_params=pltpu.CompilerParams(vmem_limit_bytes=24 * 2**20),
        cost_estimate=cost(12),
    )
    return lambda *args: run(*args)[:6]


def on_device(object_tiles, probe_modes, offsets, amplitude):
    rows, cols = object_tiles.shape[2:]
    ext_rows = rows + 2 * HALO
    scans = offsets.shape[2]
    tile = object_tiles.reshape(PLANES, rows, cols)
    offset_pairs = jnp.swapaxes(offsets, 2, 3).reshape(2, scans)
    amp = amplitude.reshape(scans, WIN, WIN)
    flat = (2 * MODES * WIN, WIN)
    mats = jnp.asarray(matrices())
    devices = lax.axis_size("row") * lax.axis_size("col")

    north = moved(tile[:, rows - HALO :], "row", 1)
    south = moved(tile[:, :HALO], "row", -1)
    east_send, west_send = call(pack_kernel, [f32(rows, LANES)] * 2, 1, us=1)(tile)
    from_west = moved(east_send, "col", 1)
    from_east = moved(west_send, "col", -1)
    east_send, west_send = call(corner_kernel, [f32(2 * HALO, LANES)] * 2, 2, us=1)(north, south)
    west_corners = moved(east_send, "col", 1)
    east_corners = moved(west_send, "col", -1)

    ext = call(assemble_kernel, f32(PLANES, 3, ext_rows, LANES), 3, us=4)(tile, north, south)
    probe_grad, center, north_rim, south_rim, east_rim, west_rim = main_call(scans, rows, cols)(
        offset_pairs, ext, from_west, from_east, west_corners, east_corners, amp, probe_modes, mats
    )

    parts = lax.all_to_all(probe_grad.reshape(devices, -1, LANES), BOTH, 0, 0, tiled=True)
    rim_from_west = moved(east_rim, "col", 1)
    rim_from_east = moved(west_rim, "col", -1)
    from_south = moved(north_rim, "row", -1)
    from_north = moved(south_rim, "row", 1)
    share = call(share_kernel, f32(*parts.shape), 1)(parts)
    total = lax.all_to_all(share, BOTH, 0, 0, tiled=True)
    to_north, to_south = call(rim_corner_kernel, [f32(2 * HALO, LANES)] * 2, 2, us=20)(rim_from_west, rim_from_east)
    south_corners = moved(to_north, "row", -1)
    north_corners = moved(to_south, "row", 1)
    object_grad = call(object_kernel, f32(PLANES, rows, cols), 7)(
        center, from_north, from_south, rim_from_west, rim_from_east, north_corners, south_corners
    )
    probe_new = call(probe_kernel, f32(*flat), 2)(total.reshape(flat), probe_modes.reshape(flat))
    return object_grad.reshape(object_tiles.shape), probe_new.reshape(probe_modes.shape)


def solution(mesh):
    placed = (
        P(None, None, "row", "col"),
        P(),
        P("row", "col", None, None),
        P("row", "col", None, None, None),
    )
    return jax.shard_map(
        on_device,
        mesh=mesh,
        in_specs=placed,
        out_specs=(P(None, None, "row", "col"), P()),
        check_vma=False,
    )
```

```python
import jax
import jax.numpy as jnp
import numpy as np
from jax import lax
from jax.experimental import pallas as pl
from jax.experimental.pallas import tpu as pltpu
from jax.sharding import PartitionSpec as P

HALO = 32
WIN = 128
MODES = 4
PLANES = 4
LANES = 128
PROP = 0.002
SHIFT_AMP = 0.5
STEP_SIZE = 0.5
EPSILON = 1e-06
BOTH = ("row", "col")


def matrices():
    k = np.arange(WIN)
    c = np.exp(-2j * np.pi * (np.outer(k, k) % WIN) / WIN) / np.sqrt(WIN)
    f = ((k + WIN // 2) % WIN - WIN // 2).astype(np.float64)
    g = c.conj() @ np.diag(np.exp(-1j * PROP * f * f)) @ c
    stack = []
    for m in (c, c.conj(), g, g.conj()):
        w = np.block([[m.real, m.imag], [-m.imag, m.real]]).astype(np.float32)
        high = w.astype(jnp.bfloat16)
        low = (w - high.astype(np.float32)).astype(jnp.bfloat16)
        stack.append(np.stack([high, low]))
    return np.stack(stack)


C, C_CONJ, G, G_CONJ = range(4)
BLOCKS = 2
ROWS = 2 * WIN // BLOCKS
CHUNKS = 4


def lane_iota(rows):
    return lax.broadcasted_iota(jnp.int32, (rows, LANES), 1)


def edges(src, rows):
    lane = lane_iota(rows)
    east = jnp.zeros((rows, LANES), jnp.float32)
    west = jnp.zeros((rows, LANES), jnp.float32)
    for p in range(PLANES):
        here = (lane >= p * HALO) & (lane < (p + 1) * HALO)
        east = jnp.where(here, turned(src[p, :, LANES : 2 * LANES], (p - 3) * HALO), east)
        west = jnp.where(here, turned(src[p, :, 0:LANES], p * HALO), west)
    return east, west


def turned(block, shift):
    return pltpu.roll(block, shift % LANES, 1) if shift % LANES else block


def pack_kernel(tile_ref, east_ref, west_ref):
    east_ref[...], west_ref[...] = edges(tile_ref, tile_ref.shape[1])


def corner_kernel(north_ref, south_ref, east_ref, west_ref):
    east_ref[0:HALO, :], west_ref[0:HALO, :] = edges(north_ref, HALO)
    east_ref[HALO:, :], west_ref[HALO:, :] = edges(south_ref, HALO)


def split(value):
    high = value.astype(jnp.bfloat16)
    return high, (value - high.astype(jnp.float32)).astype(jnp.bfloat16)


def dot(left, right):
    return jnp.dot(left, right, preferred_element_type=jnp.float32)


def assemble_kernel(tile_ref, north_ref, south_ref, ext):
    rows = tile_ref.shape[1]
    for p in range(PLANES):
        for q in range(2):
            cols = slice(q * LANES, (q + 1) * LANES)
            ext[p, q, 0:HALO, :] = north_ref[p, :, cols]
            ext[p, q, HALO : HALO + rows, :] = tile_ref[p, :, cols]
            ext[p, q, HALO + rows :, :] = south_ref[p, :, cols]


def place(offsets_ref, s, q_count=3):
    start = lax.rem(offsets_ref[1, s] + (q_count * LANES - HALO), q_count * LANES)
    first = lax.div(start, LANES)
    return offsets_ref[0, s], first, lax.rem(first + 1, q_count), lax.rem(start, LANES)


def main_kernel(
    offsets_ref, ext_in, from_west_ref, from_east_ref, west_corners_ref, east_corners_ref, amp_ref, probe_ref, mat_ref,
    probe_grad_ref, center_ref, north_rim_ref, south_rim_ref, east_rim_ref, west_rim_ref, ext,
    rh, rl, lh, ll, field, d_keep, win, factor, grad,
):
    del ext_in
    ext_rows = ext.shape[2]
    last = ext_rows - HALO

    def beside(left, right, p):
        low = lane_iota(left.shape[0]) < 2 * HALO
        return jnp.where(low, turned(right, -p * HALO), turned(left, (3 - p) * HALO))

    for p in range(PLANES):
        ext[p, 2, 0:HALO, :] = beside(west_corners_ref[0:HALO, :], east_corners_ref[0:HALO, :], p)
        ext[p, 2, HALO:last, :] = beside(from_west_ref[...], from_east_ref[...], p)
        ext[p, 2, last:ext_rows, :] = beside(west_corners_ref[HALO:, :], east_corners_ref[HALO:, :], p)

    lane = lane_iota(WIN)
    chains = range(MODES // 2)
    scans = range(amp_ref.shape[0])

    def put(high, low, at, value):
        high[at], low[at] = split(value)

    def run(*accs):
        def blocks(s, c):
            first = (s * len(chains) + c) * BLOCKS
            return accs[first : first + BLOCKS]

        def multiply(s, c, rhs, lhss, stage):
            pltpu.matmul_push_rhs(rhs, stage, c)
            for lhs in lhss:
                for b, acc in enumerate(blocks(s, c)):
                    pltpu.matmul_acc_lhs(acc, lhs[b * ROWS : (b + 1) * ROWS, :], stage)
                    stage = None

        def start_right(s, which):
            for c in chains:
                multiply(s, c, mat_ref[which, 0], (rh[s, c], rl[s, c]), 0)
                multiply(s, c, mat_ref[which, 1], (rh[s, c],), 1)

        def start_left(s, which):
            high, low = mat_ref[which ^ 1, 0], mat_ref[which ^ 1, 1]
            for c in chains:
                multiply(s, c, lh[s, c], (high, low), 0)
                multiply(s, c, ll[s, c], (high,), 1)

        def planes_right(s):
            for c in chains:
                out = jnp.concatenate([pltpu.matmul_pop(acc) for acc in blocks(s, c)], axis=0)
                for k in range(2):
                    yield c, k, out[k * WIN : (k + 1) * WIN, 0:WIN], out[k * WIN : (k + 1) * WIN, WIN:]

        def planes_left(s):
            for c in chains:
                out = jnp.concatenate([pltpu.matmul_pop(acc) for acc in blocks(s, c)], axis=0)
                for k in range(2):
                    yield c, k, out[0:WIN, k * WIN : (k + 1) * WIN], out[WIN:, k * WIN : (k + 1) * WIN]

        def put_r(s, c, k, real, imag):
            rows = slice(k * WIN, (k + 1) * WIN)
            put(rh, rl, (s, c, rows, slice(0, WIN)), real)
            put(rh, rl, (s, c, rows, slice(WIN, 2 * WIN)), imag)

        def put_l(s, c, k, real, imag):
            cols = slice(k * WIN, (k + 1) * WIN)
            put(lh, ll, (s, c, slice(0, WIN), cols), real)
            put(lh, ll, (s, c, slice(WIN, 2 * WIN), cols), imag)

        def steps(s):
            row, q, q_next, shift = place(offsets_ref, s)
            back = lax.rem(LANES - shift, LANES)

            def scatter(p, value):
                value = pltpu.roll(value, shift, 1)
                grad[p, q, pl.ds(row, WIN), :] += jnp.where(lane >= shift, value, 0.0)
                grad[p, q_next, pl.ds(row, WIN), :] += jnp.where(lane < shift, value, 0.0)

            for p in range(PLANES):
                a = pltpu.roll(ext[p, q, pl.ds(row, WIN), :], back, 1)
                b = pltpu.roll(ext[p, q_next, pl.ds(row, WIN), :], back, 1)
                win[s, p] = jnp.where(lane < LANES - shift, a, b)
            for c in chains:
                for k in range(2):
                    pr, pi = probe_ref[0, 2 * c + k], probe_ref[1, 2 * c + k]
                    put_r(s, c, k, pr * win[s, 0] - pi * win[s, 2], pr * win[s, 2] + pi * win[s, 0])
            start_right(s, G)
            if s == 0:
                grad[...] = jnp.zeros_like(grad)
            yield
            for c, k, real, imag in planes_right(s):
                put_l(s, c, k, real, imag)
            start_left(s, G)
            yield
            for c, k, real, imag in planes_left(s):
                m = 2 * c + k
                d_keep[s, 0, m] = real
                d_keep[s, 1, m] = imag
                second_r, second_i = win[s, 1], win[s, 3]
                put_l(s, c, k, real * second_r - imag * second_i, real * second_i + imag * second_r)
            start_left(s, C)
            yield
            for c, k, real, imag in planes_left(s):
                put_r(s, c, k, real, imag)
            start_right(s, C)
            yield
            intensity = jnp.full((WIN, WIN), SHIFT_AMP, jnp.float32)
            for c, k, real, imag in planes_right(s):
                m = 2 * c + k
                field[s, 0, m] = real
                field[s, 1, m] = imag
                intensity = intensity + (real * real + imag * imag)
            factor[s] = 2.0 - 2.0 * amp_ref[s] / jnp.sqrt(intensity)
            for c in chains:
                for k in range(2):
                    m = 2 * c + k
                    put_r(s, c, k, field[s, 0, m] * factor[s], field[s, 1, m] * factor[s])
            start_right(s, C_CONJ)
            yield
            for c, k, real, imag in planes_right(s):
                put_l(s, c, k, real, imag)
            start_left(s, C_CONJ)
            yield
            sum_r = jnp.zeros((WIN, WIN), jnp.float32)
            sum_i = jnp.zeros((WIN, WIN), jnp.float32)
            for c, k, real, imag in planes_left(s):
                dr, di = d_keep[s, 0, 2 * c + k], d_keep[s, 1, 2 * c + k]
                second_r, second_i = win[s, 1], win[s, 3]
                sum_r = sum_r + (dr * real + di * imag)
                sum_i = sum_i + (dr * imag - di * real)
                put_l(s, c, k, second_r * real + second_i * imag, second_r * imag - second_i * real)
            start_left(s, G_CONJ)
            scatter(1, sum_r)
            scatter(3, sum_i)
            yield
            for c, k, real, imag in planes_left(s):
                put_r(s, c, k, real, imag)
            start_right(s, G_CONJ)
            yield
            sum_r = jnp.zeros((WIN, WIN), jnp.float32)
            sum_i = jnp.zeros((WIN, WIN), jnp.float32)
            for c, k, real, imag in planes_right(s):
                m = 2 * c + k
                pr, pi = probe_ref[0, m], probe_ref[1, m]
                first_r, first_i = win[s, 0], win[s, 2]
                sum_r = sum_r + (pr * real + pi * imag)
                sum_i = sum_i + (pr * imag - pi * real)
                grad_r = first_r * real + first_i * imag
                grad_i = first_r * imag - first_i * real
                probe_grad_ref[0, m] = grad_r if s == 0 else probe_grad_ref[0, m] + grad_r
                probe_grad_ref[1, m] = grad_i if s == 0 else probe_grad_ref[1, m] + grad_i
            scatter(0, sum_r)
            scatter(2, sum_i)

        under_way = [steps(s) for s in scans]
        while under_way:
            under_way = [step for step in under_way if next(step, True) is None]

    pl.run_scoped(
        run, *[pltpu.ACC(c)((ROWS, 2 * WIN), jnp.float32) for _ in scans for c in chains for _ in range(BLOCKS)]
    )

    lane_all = lane_iota(ext_rows)
    east = jnp.zeros((ext_rows, LANES), jnp.float32)
    west = jnp.zeros((ext_rows, LANES), jnp.float32)
    for p in range(PLANES):
        for q in range(2):
            cols = slice(q * LANES, (q + 1) * LANES)
            north_rim_ref[p, :, cols] = grad[p, q, 0:HALO, :]
            center_ref[p, :, cols] = grad[p, q, HALO:last, :]
            south_rim_ref[p, :, cols] = grad[p, q, last:ext_rows, :]
        third = grad[p, 2]
        here = (lane_all >= p * HALO) & (lane_all < (p + 1) * HALO)
        east = jnp.where(here, turned(third, p * HALO), east)
        west = jnp.where(here, turned(third, (p - 3) * HALO), west)
    east_rim_ref[...] = east
    west_rim_ref[...] = west


def rim_corner_kernel(from_west_ref, from_east_ref, to_north_ref, to_south_ref):
    for k, ref in enumerate((from_west_ref, from_east_ref)):
        to_north_ref[k * HALO : (k + 1) * HALO, :] = ref[0:HALO, :]
        to_south_ref[k * HALO : (k + 1) * HALO, :] = ref[ref.shape[0] - HALO :, :]


def share_kernel(parts_ref, *refs):
    share_ref = refs[-1]
    share_ref[...] = jnp.broadcast_to(jnp.sum(parts_ref[...], axis=0)[None], share_ref.shape)


def from_sides(left, right, p):
    lane = lane_iota(left.shape[0])
    return (
        jnp.where(lane < HALO, turned(left, -p * HALO), 0.0),
        jnp.where(lane >= LANES - HALO, turned(right, (3 - p) * HALO), 0.0),
    )


def object_kernel(
    center_ref, from_north_ref, from_south_ref, from_west_ref, from_east_ref, object_ref, north_ref, south_ref
):
    rows = center_ref.shape[1]
    for p in range(PLANES):
        sides = from_sides(from_west_ref[HALO : HALO + rows, :], from_east_ref[HALO : HALO + rows, :], p)
        for q in range(2):
            cols = slice(q * LANES, (q + 1) * LANES)
            whole = center_ref[p, :, cols] + sides[q]
            object_ref[p, :, cols] = whole
            north_ref[p, :, cols] = whole[0:HALO] + from_north_ref[p, :, cols]
            south_ref[p, :, cols] = whole[rows - HALO :] + from_south_ref[p, :, cols]


def final_kernel(
    object_in, north_ref, south_ref, north_corners_ref, south_corners_ref, total_ref, probe_ref,
    object_ref, probe_new_ref, strips, steps, sem,
):
    del object_in
    rows = object_ref.shape[1]
    copies = []
    for k, (edge_ref, corners_ref) in enumerate(((north_ref, north_corners_ref), (south_ref, south_corners_ref))):
        for p in range(PLANES):
            corners = from_sides(corners_ref[0:HALO, :], corners_ref[HALO:, :], p)
            for q in range(2):
                cols = slice(q * LANES, (q + 1) * LANES)
                strips[k, p, :, cols] = edge_ref[p, :, cols] + corners[q]
        place_at = slice(0, HALO) if k == 0 else slice(rows - HALO, rows)
        copies.append(pltpu.make_async_copy(strips.at[k], object_ref.at[:, place_at, :], sem.at[k]))
        copies[-1].start()
    total = total_ref[...]
    squares = jnp.sum(total * total, axis=0, keepdims=True)
    mean = jnp.sum(squares, axis=1, keepdims=True) / (total.shape[0] * total.shape[1])
    scale = STEP_SIZE / jnp.sqrt(mean + EPSILON)
    chunk = total.shape[0] // CHUNKS
    for k in range(CHUNKS):
        part = slice(k * chunk, (k + 1) * chunk)
        steps[part, :] = probe_ref[part, :] - total_ref[part, :] * scale
        copies.append(pltpu.make_async_copy(steps.at[part, :], probe_new_ref.at[part, :], sem.at[2 + k]))
        copies[-1].start()
    for copy in copies:
        copy.wait()


def vmem(count):
    return [pl.BlockSpec(memory_space=pltpu.VMEM)] * count


def f32(*shape):
    return jax.ShapeDtypeStruct(shape, jnp.float32)


def moved(block, axis, distance):
    count = lax.axis_size(axis)
    return lax.ppermute(block, axis, [(i, (i + distance) % count) for i in range(count)])


def cost(us):
    return pl.CostEstimate(flops=int(us * 1e9), bytes_accessed=int(us * 3e6), transcendentals=0)


def call(kernel, outs, ins, scratch=(), scalars=0, limit=2, us=0):
    return pl.pallas_call(
        kernel,
        out_shape=outs,
        in_specs=[pl.BlockSpec(memory_space=pltpu.SMEM)] * scalars + vmem(ins),
        out_specs=vmem(len(outs)) if isinstance(outs, list) else vmem(1)[0],
        scratch_shapes=scratch,
        compiler_params=pltpu.CompilerParams(vmem_limit_bytes=limit * 2**20),
        cost_estimate=cost(us) if us else None,
    )


def main_call(scans, rows, cols):
    ext_rows = rows + 2 * HALO
    pair = pltpu.VMEM((scans, MODES // 2, 2 * WIN, 2 * WIN), jnp.bfloat16)
    modes = pltpu.VMEM((scans, 2, MODES, WIN, WIN), jnp.float32)
    outs = [f32(2, MODES, WIN, WIN), f32(PLANES, rows, cols)]
    outs += [f32(PLANES, HALO, cols)] * 2 + [f32(ext_rows, LANES)] * 2 + [f32(PLANES, 3, ext_rows, LANES)]
    run = pl.pallas_call(
        main_kernel,
        out_shape=outs,
        in_specs=[pl.BlockSpec(memory_space=pltpu.SMEM)] + vmem(8),
        out_specs=vmem(len(outs)),
        scratch_shapes=[
            pair, pair, pair, pair, modes, modes,
            pltpu.VMEM((scans, PLANES, WIN, WIN), jnp.float32),
            pltpu.VMEM((scans, WIN, WIN), jnp.float32),
            pltpu.VMEM((PLANES, 3, ext_rows, LANES), jnp.float32),
        ],
        input_output_aliases={1: 6},
        compiler_params=pltpu.CompilerParams(vmem_limit_bytes=24 * 2**20),
        cost_estimate=cost(12),
    )
    return lambda *args: run(*args)[:6]


def on_device(object_tiles, probe_modes, offsets, amplitude):
    rows, cols = object_tiles.shape[2:]
    ext_rows = rows + 2 * HALO
    scans = offsets.shape[2]
    tile = object_tiles.reshape(PLANES, rows, cols)
    offset_pairs = jnp.swapaxes(offsets, 2, 3).reshape(2, scans)
    amp = amplitude.reshape(scans, WIN, WIN)
    flat = (2 * MODES * WIN, WIN)
    mats = jnp.asarray(matrices())
    devices = lax.axis_size("row") * lax.axis_size("col")

    north = moved(tile[:, rows - HALO :], "row", 1)
    south = moved(tile[:, :HALO], "row", -1)
    east_send, west_send = call(pack_kernel, [f32(rows, LANES)] * 2, 1, us=1)(tile)
    from_west = moved(east_send, "col", 1)
    from_east = moved(west_send, "col", -1)
    east_send, west_send = call(corner_kernel, [f32(2 * HALO, LANES)] * 2, 2, us=1)(north, south)
    west_corners = moved(east_send, "col", 1)
    east_corners = moved(west_send, "col", -1)

    ext = call(assemble_kernel, f32(PLANES, 3, ext_rows, LANES), 3, us=4)(tile, north, south)
    probe_grad, center, north_rim, south_rim, east_rim, west_rim = main_call(scans, rows, cols)(
        offset_pairs, ext, from_west, from_east, west_corners, east_corners, amp, probe_modes, mats
    )

    parts = lax.all_to_all(probe_grad.reshape(devices, -1, LANES), BOTH, 0, 0, tiled=True)
    rim_from_west = moved(east_rim, "col", 1)
    rim_from_east = moved(west_rim, "col", -1)
    from_south = moved(north_rim, "row", -1)
    from_north = moved(south_rim, "row", 1)
    share = call(share_kernel, f32(*parts.shape), 1)(parts)
    total = lax.all_to_all(share, BOTH, 0, 0, tiled=True)
    to_north, to_south = call(rim_corner_kernel, [f32(2 * HALO, LANES)] * 2, 2, us=20)(rim_from_west, rim_from_east)
    south_corners = moved(to_north, "row", -1)
    north_corners = moved(to_south, "row", 1)
    edge = f32(PLANES, HALO, cols)
    bulk, north_edge, south_edge = call(object_kernel, [f32(PLANES, rows, cols), edge, edge], 5)(
        center, from_north, from_south, rim_from_west, rim_from_east
    )
    anywhere = pl.BlockSpec(memory_space=pl.ANY)
    object_grad, probe_new = pl.pallas_call(
        final_kernel,
        out_shape=[f32(PLANES, rows, cols), f32(*flat)],
        in_specs=[anywhere] + vmem(6),
        out_specs=[anywhere] * 2,
        scratch_shapes=[
            pltpu.VMEM((2, PLANES, HALO, cols), jnp.float32),
            pltpu.VMEM(flat, jnp.float32),
            pltpu.SemaphoreType.DMA((2 + CHUNKS,)),
        ],
        input_output_aliases={0: 0},
        compiler_params=pltpu.CompilerParams(vmem_limit_bytes=2 * 2**20),
    )(
        bulk, north_edge, south_edge, north_corners, south_corners, total.reshape(flat), probe_modes.reshape(flat)
    )
    return object_grad.reshape(object_tiles.shape), probe_new.reshape(probe_modes.shape)


def solution(mesh):
    placed = (
        P(None, None, "row", "col"),
        P(),
        P("row", "col", None, None),
        P("row", "col", None, None, None),
    )
    return jax.shard_map(
        on_device,
        mesh=mesh,
        in_specs=placed,
        out_specs=(P(None, None, "row", "col"), P()),
        check_vma=False,
    )
```

```python
import math

import jax
import jax.numpy as jnp
import numpy as np
from jax import lax
from jax.experimental import pallas as pl
from jax.experimental.pallas import tpu as pltpu
from jax.sharding import PartitionSpec as P

HALO = 32
WIN = 128
MODES = 4
PLANES = 4
LANES = 128
PROP = 0.002
SHIFT_AMP = 0.5
STEP_SIZE = 0.5
EPSILON = 1e-06
COL = ("pair", "core")
PEERS = ("row", "pair")
SWAP = [(0, 1), (1, 0)]


def matrices():
    k = np.arange(WIN)
    c = np.exp(-2j * np.pi * (np.outer(k, k) % WIN) / WIN) / np.sqrt(WIN)
    f = ((k + WIN // 2) % WIN - WIN // 2).astype(np.float64)
    g = c.conj() @ np.diag(np.exp(-1j * PROP * f * f)) @ c
    stack = []
    for m in (c, c.conj(), g, g.conj()):
        w = np.block([[m.real, m.imag], [-m.imag, m.real]]).astype(np.float32)
        high = w.astype(jnp.bfloat16)
        low = (w - high.astype(np.float32)).astype(jnp.bfloat16)
        stack.append(np.stack([high, low]))
    return np.stack(stack)


C, C_CONJ, G, G_CONJ = range(4)
BLOCKS = 2
ROWS = 2 * WIN // BLOCKS
CHUNKS = 4


def lane_iota(rows):
    return lax.broadcasted_iota(jnp.int32, (rows, LANES), 1)


def edges(src, rows):
    lane = lane_iota(rows)
    east = jnp.zeros((rows, LANES), jnp.float32)
    west = jnp.zeros((rows, LANES), jnp.float32)
    for p in range(PLANES):
        here = (lane >= p * HALO) & (lane < (p + 1) * HALO)
        east = jnp.where(here, turned(src[p, :, LANES : 2 * LANES], (p - 3) * HALO), east)
        west = jnp.where(here, turned(src[p, :, 0:LANES], p * HALO), west)
    return east, west


def turned(block, shift):
    return pltpu.roll(block, shift % LANES, 1) if shift % LANES else block


def pack_kernel(tile_ref, east_ref, west_ref):
    east_ref[...], west_ref[...] = edges(tile_ref, tile_ref.shape[1])


def corner_kernel(north_ref, south_ref, east_ref, west_ref):
    east_ref[0:HALO, :], west_ref[0:HALO, :] = edges(north_ref, HALO)
    east_ref[HALO:, :], west_ref[HALO:, :] = edges(south_ref, HALO)


def split(value):
    high = value.astype(jnp.bfloat16)
    return high, (value - high.astype(jnp.float32)).astype(jnp.bfloat16)


def dot(left, right):
    return jnp.dot(left, right, preferred_element_type=jnp.float32)


def assemble_kernel(tile_ref, north_ref, south_ref, ext):
    rows = tile_ref.shape[1]
    for p in range(PLANES):
        for q in range(2):
            cols = slice(q * LANES, (q + 1) * LANES)
            ext[p, q, 0:HALO, :] = north_ref[p, :, cols]
            ext[p, q, HALO : HALO + rows, :] = tile_ref[p, :, cols]
            ext[p, q, HALO + rows :, :] = south_ref[p, :, cols]


def place(offsets_ref, s, q_count=3):
    start = lax.rem(offsets_ref[1, s] + (q_count * LANES - HALO), q_count * LANES)
    first = lax.div(start, LANES)
    return offsets_ref[0, s], first, lax.rem(first + 1, q_count), lax.rem(start, LANES)


def main_kernel(
    offsets_ref, core_ref, ext_in, from_west_ref, from_east_ref, west_corners_ref, east_corners_ref, amp_ref, probe_ref, mat_ref,
    keep_ref, send_ref, center_ref, north_rim_ref, south_rim_ref, east_rim_ref, west_rim_ref, ext,
    rh, rl, lh, ll, field, d_keep, win, factor, grad, probe_grad_ref,
):
    del ext_in
    ext_rows = ext.shape[2]
    last = ext_rows - HALO

    def beside(left, right, p):
        low = lane_iota(left.shape[0]) < 2 * HALO
        return jnp.where(low, turned(right, -p * HALO), turned(left, (3 - p) * HALO))

    for p in range(PLANES):
        ext[p, 2, 0:HALO, :] = beside(west_corners_ref[0:HALO, :], east_corners_ref[0:HALO, :], p)
        ext[p, 2, HALO:last, :] = beside(from_west_ref[...], from_east_ref[...], p)
        ext[p, 2, last:ext_rows, :] = beside(west_corners_ref[HALO:, :], east_corners_ref[HALO:, :], p)

    lane = lane_iota(WIN)
    chains = range(MODES // 2)
    scans = range(amp_ref.shape[0])

    def put(high, low, at, value):
        high[at], low[at] = split(value)

    def run(*accs):
        def blocks(s, c):
            first = (s * len(chains) + c) * BLOCKS
            return accs[first : first + BLOCKS]

        def multiply(s, c, rhs, lhss, stage):
            pltpu.matmul_push_rhs(rhs, stage, c)
            for lhs in lhss:
                for b, acc in enumerate(blocks(s, c)):
                    pltpu.matmul_acc_lhs(acc, lhs[b * ROWS : (b + 1) * ROWS, :], stage)
                    stage = None

        def start_right(s, which):
            for c in chains:
                multiply(s, c, mat_ref[which, 0], (rh[s, c], rl[s, c]), 0)
                multiply(s, c, mat_ref[which, 1], (rh[s, c],), 1)

        def start_left(s, which):
            high, low = mat_ref[which ^ 1, 0], mat_ref[which ^ 1, 1]
            for c in chains:
                multiply(s, c, lh[s, c], (high, low), 0)
                multiply(s, c, ll[s, c], (high,), 1)

        def planes_right(s):
            for c in chains:
                out = jnp.concatenate([pltpu.matmul_pop(acc) for acc in blocks(s, c)], axis=0)
                for k in range(2):
                    yield c, k, out[k * WIN : (k + 1) * WIN, 0:WIN], out[k * WIN : (k + 1) * WIN, WIN:]

        def planes_left(s):
            for c in chains:
                out = jnp.concatenate([pltpu.matmul_pop(acc) for acc in blocks(s, c)], axis=0)
                for k in range(2):
                    yield c, k, out[0:WIN, k * WIN : (k + 1) * WIN], out[WIN:, k * WIN : (k + 1) * WIN]

        def put_r(s, c, k, real, imag):
            rows = slice(k * WIN, (k + 1) * WIN)
            put(rh, rl, (s, c, rows, slice(0, WIN)), real)
            put(rh, rl, (s, c, rows, slice(WIN, 2 * WIN)), imag)

        def put_l(s, c, k, real, imag):
            cols = slice(k * WIN, (k + 1) * WIN)
            put(lh, ll, (s, c, slice(0, WIN), cols), real)
            put(lh, ll, (s, c, slice(WIN, 2 * WIN), cols), imag)

        def steps(s):
            row, q, q_next, shift = place(offsets_ref, s)
            back = lax.rem(LANES - shift, LANES)

            def scatter(p, value):
                value = pltpu.roll(value, shift, 1)
                grad[p, q, pl.ds(row, WIN), :] += jnp.where(lane >= shift, value, 0.0)
                grad[p, q_next, pl.ds(row, WIN), :] += jnp.where(lane < shift, value, 0.0)

            for p in range(PLANES):
                a = pltpu.roll(ext[p, q, pl.ds(row, WIN), :], back, 1)
                b = pltpu.roll(ext[p, q_next, pl.ds(row, WIN), :], back, 1)
                win[s, p] = jnp.where(lane < LANES - shift, a, b)
            for c in chains:
                for k in range(2):
                    pr, pi = probe_ref[0, 2 * c + k], probe_ref[1, 2 * c + k]
                    put_r(s, c, k, pr * win[s, 0] - pi * win[s, 2], pr * win[s, 2] + pi * win[s, 0])
            start_right(s, G)
            if s == 0:
                grad[...] = jnp.zeros_like(grad)
            yield
            for c, k, real, imag in planes_right(s):
                put_l(s, c, k, real, imag)
            start_left(s, G)
            yield
            for c, k, real, imag in planes_left(s):
                m = 2 * c + k
                d_keep[s, 0, m] = real
                d_keep[s, 1, m] = imag
                second_r, second_i = win[s, 1], win[s, 3]
                put_l(s, c, k, real * second_r - imag * second_i, real * second_i + imag * second_r)
            start_left(s, C)
            yield
            for c, k, real, imag in planes_left(s):
                put_r(s, c, k, real, imag)
            start_right(s, C)
            yield
            intensity = jnp.full((WIN, WIN), SHIFT_AMP, jnp.float32)
            for c, k, real, imag in planes_right(s):
                m = 2 * c + k
                field[s, 0, m] = real
                field[s, 1, m] = imag
                intensity = intensity + (real * real + imag * imag)
            factor[s] = 2.0 - 2.0 * amp_ref[s] / jnp.sqrt(intensity)
            for c in chains:
                for k in range(2):
                    m = 2 * c + k
                    put_r(s, c, k, field[s, 0, m] * factor[s], field[s, 1, m] * factor[s])
            start_right(s, C_CONJ)
            yield
            for c, k, real, imag in planes_right(s):
                put_l(s, c, k, real, imag)
            start_left(s, C_CONJ)
            yield
            sum_r = jnp.zeros((WIN, WIN), jnp.float32)
            sum_i = jnp.zeros((WIN, WIN), jnp.float32)
            for c, k, real, imag in planes_left(s):
                dr, di = d_keep[s, 0, 2 * c + k], d_keep[s, 1, 2 * c + k]
                second_r, second_i = win[s, 1], win[s, 3]
                sum_r = sum_r + (dr * real + di * imag)
                sum_i = sum_i + (dr * imag - di * real)
                put_l(s, c, k, second_r * real + second_i * imag, second_r * imag - second_i * real)
            start_left(s, G_CONJ)
            scatter(1, sum_r)
            scatter(3, sum_i)
            yield
            for c, k, real, imag in planes_left(s):
                put_r(s, c, k, real, imag)
            start_right(s, G_CONJ)
            yield
            sum_r = jnp.zeros((WIN, WIN), jnp.float32)
            sum_i = jnp.zeros((WIN, WIN), jnp.float32)
            for c, k, real, imag in planes_right(s):
                m = 2 * c + k
                pr, pi = probe_ref[0, m], probe_ref[1, m]
                first_r, first_i = win[s, 0], win[s, 2]
                sum_r = sum_r + (pr * real + pi * imag)
                sum_i = sum_i + (pr * imag - pi * real)
                grad_r = first_r * real + first_i * imag
                grad_i = first_r * imag - first_i * real
                probe_grad_ref[0, m] = grad_r if s == 0 else probe_grad_ref[0, m] + grad_r
                probe_grad_ref[1, m] = grad_i if s == 0 else probe_grad_ref[1, m] + grad_i
            scatter(0, sum_r)
            scatter(2, sum_i)

        under_way = [steps(s) for s in scans]
        while under_way:
            under_way = [step for step in under_way if next(step, True) is None]

    pl.run_scoped(
        run, *[pltpu.ACC(c)((ROWS, 2 * WIN), jnp.float32) for _ in scans for c in chains for _ in range(BLOCKS)]
    )

    keep_ref[...] = probe_grad_ref[core_ref[0]]
    send_ref[...] = probe_grad_ref[1 - core_ref[0]]
    lane_all = lane_iota(ext_rows)
    east = jnp.zeros((ext_rows, LANES), jnp.float32)
    west = jnp.zeros((ext_rows, LANES), jnp.float32)
    for p in range(PLANES):
        for q in range(2):
            cols = slice(q * LANES, (q + 1) * LANES)
            north_rim_ref[p, :, cols] = grad[p, q, 0:HALO, :]
            center_ref[p, :, cols] = grad[p, q, HALO:last, :]
            south_rim_ref[p, :, cols] = grad[p, q, last:ext_rows, :]
        third = grad[p, 2]
        here = (lane_all >= p * HALO) & (lane_all < (p + 1) * HALO)
        east = jnp.where(here, turned(third, p * HALO), east)
        west = jnp.where(here, turned(third, (p - 3) * HALO), west)
    east_rim_ref[...] = east
    west_rim_ref[...] = west


def rim_corner_kernel(from_west_ref, from_east_ref, to_north_ref, to_south_ref):
    for k, ref in enumerate((from_west_ref, from_east_ref)):
        to_north_ref[k * HALO : (k + 1) * HALO, :] = ref[0:HALO, :]
        to_south_ref[k * HALO : (k + 1) * HALO, :] = ref[ref.shape[0] - HALO :, :]


def add_kernel(left_ref, right_ref, out_ref):
    out_ref[...] = left_ref[...] + right_ref[...]


def share_kernel(parts_ref, *refs):
    share_ref = refs[-1]
    share_ref[...] = jnp.broadcast_to(jnp.sum(parts_ref[...], axis=0)[None], share_ref.shape)


def from_sides(left, right, p):
    lane = lane_iota(left.shape[0])
    return (
        jnp.where(lane < HALO, turned(left, -p * HALO), 0.0),
        jnp.where(lane >= LANES - HALO, turned(right, (3 - p) * HALO), 0.0),
    )


def object_kernel(
    center_ref, from_north_ref, from_south_ref, from_west_ref, from_east_ref, object_ref, north_ref, south_ref
):
    rows = center_ref.shape[1]
    for p in range(PLANES):
        sides = from_sides(from_west_ref[HALO : HALO + rows, :], from_east_ref[HALO : HALO + rows, :], p)
        for q in range(2):
            cols = slice(q * LANES, (q + 1) * LANES)
            whole = center_ref[p, :, cols] + sides[q]
            object_ref[p, :, cols] = whole
            north_ref[p, :, cols] = whole[0:HALO] + from_north_ref[p, :, cols]
            south_ref[p, :, cols] = whole[rows - HALO :] + from_south_ref[p, :, cols]


def final_kernel(
    object_in, north_ref, south_ref, north_corners_ref, south_corners_ref, mine_ref, other_ref, probe_ref, core_ref,
    object_ref, probe_new_ref, strips, steps, sem,
):
    del object_in
    rows = object_ref.shape[1]
    copies = []
    for k, (edge_ref, corners_ref) in enumerate(((north_ref, north_corners_ref), (south_ref, south_corners_ref))):
        for p in range(PLANES):
            corners = from_sides(corners_ref[0:HALO, :], corners_ref[HALO:, :], p)
            for q in range(2):
                cols = slice(q * LANES, (q + 1) * LANES)
                strips[k, p, :, cols] = edge_ref[p, :, cols] + corners[q]
        place_at = slice(0, HALO) if k == 0 else slice(rows - HALO, rows)
        copies.append(pltpu.make_async_copy(strips.at[k], object_ref.at[:, place_at, :], sem.at[k]))
        copies[-1].start()
    squares = jnp.sum(mine_ref[...] * mine_ref[...] + other_ref[...] * other_ref[...], axis=0, keepdims=True)
    mean = jnp.sum(squares, axis=1, keepdims=True) / (2 * mine_ref.shape[0] * mine_ref.shape[1])
    scale = STEP_SIZE / jnp.sqrt(mean + EPSILON)
    core = core_ref[0]
    chunk = mine_ref.shape[0] // CHUNKS
    for k in range(CHUNKS):
        part = slice(k * chunk, (k + 1) * chunk)
        steps[core, part, :] = probe_ref[core, part, :] - mine_ref[part, :] * scale
        steps[1 - core, part, :] = probe_ref[1 - core, part, :] - other_ref[part, :] * scale
        copies.append(pltpu.make_async_copy(steps.at[:, part, :], probe_new_ref.at[:, part, :], sem.at[2 + k]))
        copies[-1].start()
    for copy in copies:
        copy.wait()


def vmem(count):
    return [pl.BlockSpec(memory_space=pltpu.VMEM)] * count


def f32(*shape):
    return jax.ShapeDtypeStruct(shape, jnp.float32)


def axis_count(axes):
    return math.prod(lax.axis_size(a) for a in ((axes,) if isinstance(axes, str) else axes))


def moved(block, axis, distance):
    count = axis_count(axis)
    return lax.ppermute(block, axis, [(i, (i + distance) % count) for i in range(count)])


def cost(us):
    return pl.CostEstimate(flops=int(us * 1e9), bytes_accessed=int(us * 3e6), transcendentals=0)


def call(kernel, outs, ins, scratch=(), scalars=0, limit=2, us=0):
    return pl.pallas_call(
        kernel,
        out_shape=outs,
        in_specs=[pl.BlockSpec(memory_space=pltpu.SMEM)] * scalars + vmem(ins),
        out_specs=vmem(len(outs)) if isinstance(outs, list) else vmem(1)[0],
        scratch_shapes=scratch,
        compiler_params=pltpu.CompilerParams(vmem_limit_bytes=limit * 2**20),
        cost_estimate=cost(us) if us else None,
    )


def main_call(scans, rows, cols):
    ext_rows = rows + 2 * HALO
    pair = pltpu.VMEM((scans, MODES // 2, 2 * WIN, 2 * WIN), jnp.bfloat16)
    modes = pltpu.VMEM((scans, 2, MODES, WIN, WIN), jnp.float32)
    outs = [f32(MODES, WIN, WIN), f32(MODES, WIN, WIN), f32(PLANES, rows, cols)]
    outs += [f32(PLANES, HALO, cols)] * 2 + [f32(ext_rows, LANES)] * 2 + [f32(PLANES, 3, ext_rows, LANES)]
    run = pl.pallas_call(
        main_kernel,
        out_shape=outs,
        in_specs=[pl.BlockSpec(memory_space=pltpu.SMEM)] * 2 + vmem(8),
        out_specs=vmem(len(outs)),
        scratch_shapes=[
            pair, pair, pair, pair, modes, modes,
            pltpu.VMEM((scans, PLANES, WIN, WIN), jnp.float32),
            pltpu.VMEM((scans, WIN, WIN), jnp.float32),
            pltpu.VMEM((PLANES, 3, ext_rows, LANES), jnp.float32),
            pltpu.VMEM((2, MODES, WIN, WIN), jnp.float32),
        ],
        input_output_aliases={2: 7},
        compiler_params=pltpu.CompilerParams(vmem_limit_bytes=24 * 2**20),
        cost_estimate=cost(12),
    )
    return lambda *args: run(*args)[:7]


def on_device(object_tiles, probe_modes, offsets, amplitude):
    rows, cols = object_tiles.shape[2:]
    ext_rows = rows + 2 * HALO
    scans = offsets.shape[2]
    tile = object_tiles.reshape(PLANES, rows, cols)
    core = lax.axis_index("core").astype(jnp.int32).reshape(1)
    offset_pairs = jnp.swapaxes(offsets, 2, 3).reshape(2, scans)
    amp = amplitude.reshape(scans, WIN, WIN)
    flat = (2, MODES * WIN, WIN)
    mats = jnp.asarray(matrices())

    north = moved(tile[:, rows - HALO :], "row", 1)
    south = moved(tile[:, :HALO], "row", -1)
    east_send, west_send = call(pack_kernel, [f32(rows, LANES)] * 2, 1, us=1)(tile)
    from_west = moved(east_send, COL, 1)
    from_east = moved(west_send, COL, -1)
    east_send, west_send = call(corner_kernel, [f32(2 * HALO, LANES)] * 2, 2, us=1)(north, south)
    west_corners = moved(east_send, COL, 1)
    east_corners = moved(west_send, COL, -1)

    ext = call(assemble_kernel, f32(PLANES, 3, ext_rows, LANES), 3, us=4)(tile, north, south)
    keep, send, center, north_rim, south_rim, east_rim, west_rim = main_call(scans, rows, cols)(
        offset_pairs, core, ext, from_west, from_east, west_corners, east_corners, amp, probe_modes, mats
    )

    got = lax.ppermute(send, "core", SWAP)
    half_sum = call(add_kernel, f32(MODES, WIN, WIN), 2)(keep, got)
    parts = lax.all_to_all(half_sum.reshape(axis_count(PEERS), -1, LANES), PEERS, 0, 0, tiled=True)
    rim_from_west = moved(east_rim, COL, 1)
    rim_from_east = moved(west_rim, COL, -1)
    from_south = moved(north_rim, "row", -1)
    from_north = moved(south_rim, "row", 1)
    share = call(share_kernel, f32(*parts.shape), 1)(parts)
    mine = lax.all_to_all(share, PEERS, 0, 0, tiled=True).reshape(MODES * WIN, WIN)
    other = lax.ppermute(mine, "core", SWAP)
    to_north, to_south = call(rim_corner_kernel, [f32(2 * HALO, LANES)] * 2, 2, us=80)(rim_from_west, rim_from_east)
    south_corners = moved(to_north, "row", -1)
    north_corners = moved(to_south, "row", 1)
    edge = f32(PLANES, HALO, cols)
    bulk, north_edge, south_edge = call(object_kernel, [f32(PLANES, rows, cols), edge, edge], 5, us=80)(
        center, from_north, from_south, rim_from_west, rim_from_east
    )
    anywhere = pl.BlockSpec(memory_space=pl.ANY)
    object_grad, probe_new = pl.pallas_call(
        final_kernel,
        out_shape=[f32(PLANES, rows, cols), f32(*flat)],
        in_specs=[anywhere] + vmem(7) + [pl.BlockSpec(memory_space=pltpu.SMEM)],
        out_specs=[anywhere] * 2,
        scratch_shapes=[
            pltpu.VMEM((2, PLANES, HALO, cols), jnp.float32),
            pltpu.VMEM(flat, jnp.float32),
            pltpu.SemaphoreType.DMA((2 + CHUNKS,)),
        ],
        input_output_aliases={0: 0},
        compiler_params=pltpu.CompilerParams(vmem_limit_bytes=2 * 2**20),
    )(
        bulk, north_edge, south_edge, north_corners, south_corners, mine, other, probe_modes.reshape(flat), core
    )
    return object_grad.reshape(object_tiles.shape), probe_new.reshape(probe_modes.shape)


def solution(mesh):
    names = ("row",) + COL
    split_mesh = jax.sharding.Mesh(mesh.devices.reshape(mesh.shape["row"], -1, 2), names)
    placed = (
        P(None, None, "row", COL),
        P(),
        P("row", COL, None, None),
        P("row", COL, None, None, None),
    )
    return jax.shard_map(
        on_device,
        mesh=split_mesh,
        in_specs=placed,
        out_specs=(P(None, None, "row", COL), P()),
        check_vma=False,
    )
```

```python
import jax
import jax.numpy as jnp
import numpy as np
from jax import lax
from jax.experimental import pallas as pl
from jax.experimental.pallas import tpu as pltpu
from jax.sharding import PartitionSpec as P

HALO = 32
WIN = 128
MODES = 4
PLANES = 4
LANES = 128
PROP = 0.002
SHIFT_AMP = 0.5
STEP_SIZE = 0.5
EPSILON = 1e-06
BOTH = ("row", "col")


def matrices():
    k = np.arange(WIN)
    c = np.exp(-2j * np.pi * (np.outer(k, k) % WIN) / WIN) / np.sqrt(WIN)
    f = ((k + WIN // 2) % WIN - WIN // 2).astype(np.float64)
    g = c.conj() @ np.diag(np.exp(-1j * PROP * f * f)) @ c
    stack = []
    for m in (c, c.conj(), g, g.conj()):
        w = np.block([[m.real, m.imag], [-m.imag, m.real]]).astype(np.float32)
        high = w.astype(jnp.bfloat16)
        low = (w - high.astype(np.float32)).astype(jnp.bfloat16)
        stack.append(np.stack([high, low]))
    return np.stack(stack)


C, C_CONJ, G, G_CONJ = range(4)
BLOCKS = 2
ROWS = 2 * WIN // BLOCKS
CHUNKS = 4


def lane_iota(rows):
    return lax.broadcasted_iota(jnp.int32, (rows, LANES), 1)


def edges(src, rows):
    lane = lane_iota(rows)
    east = jnp.zeros((rows, LANES), jnp.float32)
    west = jnp.zeros((rows, LANES), jnp.float32)
    for p in range(PLANES):
        here = (lane >= p * HALO) & (lane < (p + 1) * HALO)
        east = jnp.where(here, turned(src[p, :, LANES : 2 * LANES], (p - 3) * HALO), east)
        west = jnp.where(here, turned(src[p, :, 0:LANES], p * HALO), west)
    return east, west


def turned(block, shift):
    return pltpu.roll(block, shift % LANES, 1) if shift % LANES else block


def pack_kernel(tile_ref, east_ref, west_ref):
    east_ref[...], west_ref[...] = edges(tile_ref, tile_ref.shape[1])


def corner_kernel(north_ref, south_ref, east_ref, west_ref):
    east_ref[0:HALO, :], west_ref[0:HALO, :] = edges(north_ref, HALO)
    east_ref[HALO:, :], west_ref[HALO:, :] = edges(south_ref, HALO)


def split(value):
    high = value.astype(jnp.bfloat16)
    return high, (value - high.astype(jnp.float32)).astype(jnp.bfloat16)


def dot(left, right):
    return jnp.dot(left, right, preferred_element_type=jnp.float32)


def assemble_kernel(tile_ref, north_ref, south_ref, ext):
    rows = tile_ref.shape[1]
    for p in range(PLANES):
        for q in range(2):
            cols = slice(q * LANES, (q + 1) * LANES)
            ext[p, q, 0:HALO, :] = north_ref[p, :, cols]
            ext[p, q, HALO : HALO + rows, :] = tile_ref[p, :, cols]
            ext[p, q, HALO + rows :, :] = south_ref[p, :, cols]


def place(offsets_ref, s, q_count=3):
    start = lax.rem(offsets_ref[1, s] + (q_count * LANES - HALO), q_count * LANES)
    first = lax.div(start, LANES)
    return offsets_ref[0, s], first, lax.rem(first + 1, q_count), lax.rem(start, LANES)


def main_kernel(
    offsets_ref, ext_in, from_west_ref, from_east_ref, west_corners_ref, east_corners_ref, amp_ref, probe_ref, mat_ref,
    probe_out_ref, center_ref, north_rim_ref, south_rim_ref, east_rim_ref, west_rim_ref, ext,
    rh, rl, lh, ll, field, d_keep, win, factor, grad, probe_grad_ref, sem,
):
    del ext_in
    ext_rows = ext.shape[2]
    last = ext_rows - HALO

    def beside(left, right, p):
        low = lane_iota(left.shape[0]) < 2 * HALO
        return jnp.where(low, turned(right, -p * HALO), turned(left, (3 - p) * HALO))

    for p in range(PLANES):
        ext[p, 2, 0:HALO, :] = beside(west_corners_ref[0:HALO, :], east_corners_ref[0:HALO, :], p)
        ext[p, 2, HALO:last, :] = beside(from_west_ref[...], from_east_ref[...], p)
        ext[p, 2, last:ext_rows, :] = beside(west_corners_ref[HALO:, :], east_corners_ref[HALO:, :], p)

    lane = lane_iota(WIN)
    chains = range(MODES // 2)
    scans = range(amp_ref.shape[0])

    def put(high, low, at, value):
        high[at], low[at] = split(value)

    def write(part, m):
        return pltpu.make_async_copy(probe_grad_ref.at[part, m], probe_out_ref.at[part, m], sem.at[part * MODES + m])

    def run(*accs):
        def blocks(s, c):
            first = (s * len(chains) + c) * BLOCKS
            return accs[first : first + BLOCKS]

        def multiply(s, c, rhs, lhss, stage):
            pltpu.matmul_push_rhs(rhs, stage, c)
            for lhs in lhss:
                for b, acc in enumerate(blocks(s, c)):
                    pltpu.matmul_acc_lhs(acc, lhs[b * ROWS : (b + 1) * ROWS, :], stage)
                    stage = None

        def start_right(s, which):
            for c in chains:
                multiply(s, c, mat_ref[which, 0], (rh[s, c], rl[s, c]), 0)
                multiply(s, c, mat_ref[which, 1], (rh[s, c],), 1)

        def start_left(s, which):
            high, low = mat_ref[which ^ 1, 0], mat_ref[which ^ 1, 1]
            for c in chains:
                multiply(s, c, lh[s, c], (high, low), 0)
                multiply(s, c, ll[s, c], (high,), 1)

        def planes_right(s):
            for c in chains:
                out = jnp.concatenate([pltpu.matmul_pop(acc) for acc in blocks(s, c)], axis=0)
                for k in range(2):
                    yield c, k, out[k * WIN : (k + 1) * WIN, 0:WIN], out[k * WIN : (k + 1) * WIN, WIN:]

        def planes_left(s):
            for c in chains:
                out = jnp.concatenate([pltpu.matmul_pop(acc) for acc in blocks(s, c)], axis=0)
                for k in range(2):
                    yield c, k, out[0:WIN, k * WIN : (k + 1) * WIN], out[WIN:, k * WIN : (k + 1) * WIN]

        def put_r(s, c, k, real, imag):
            rows = slice(k * WIN, (k + 1) * WIN)
            put(rh, rl, (s, c, rows, slice(0, WIN)), real)
            put(rh, rl, (s, c, rows, slice(WIN, 2 * WIN)), imag)

        def put_l(s, c, k, real, imag):
            cols = slice(k * WIN, (k + 1) * WIN)
            put(lh, ll, (s, c, slice(0, WIN), cols), real)
            put(lh, ll, (s, c, slice(WIN, 2 * WIN), cols), imag)

        def steps(s):
            row, q, q_next, shift = place(offsets_ref, s)
            back = lax.rem(LANES - shift, LANES)

            def scatter(p, value):
                value = pltpu.roll(value, shift, 1)
                grad[p, q, pl.ds(row, WIN), :] += jnp.where(lane >= shift, value, 0.0)
                grad[p, q_next, pl.ds(row, WIN), :] += jnp.where(lane < shift, value, 0.0)

            for p in range(PLANES):
                a = pltpu.roll(ext[p, q, pl.ds(row, WIN), :], back, 1)
                b = pltpu.roll(ext[p, q_next, pl.ds(row, WIN), :], back, 1)
                win[s, p] = jnp.where(lane < LANES - shift, a, b)
            for c in chains:
                for k in range(2):
                    pr, pi = probe_ref[0, 2 * c + k], probe_ref[1, 2 * c + k]
                    put_r(s, c, k, pr * win[s, 0] - pi * win[s, 2], pr * win[s, 2] + pi * win[s, 0])
            start_right(s, G)
            if s == 0:
                grad[...] = jnp.zeros_like(grad)
            yield
            for c, k, real, imag in planes_right(s):
                put_l(s, c, k, real, imag)
            start_left(s, G)
            yield
            for c, k, real, imag in planes_left(s):
                m = 2 * c + k
                d_keep[s, 0, m] = real
                d_keep[s, 1, m] = imag
                second_r, second_i = win[s, 1], win[s, 3]
                put_l(s, c, k, real * second_r - imag * second_i, real * second_i + imag * second_r)
            start_left(s, C)
            yield
            for c, k, real, imag in planes_left(s):
                put_r(s, c, k, real, imag)
            start_right(s, C)
            yield
            intensity = jnp.full((WIN, WIN), SHIFT_AMP, jnp.float32)
            for c, k, real, imag in planes_right(s):
                m = 2 * c + k
                field[s, 0, m] = real
                field[s, 1, m] = imag
                intensity = intensity + (real * real + imag * imag)
            factor[s] = 2.0 - 2.0 * amp_ref[s] / jnp.sqrt(intensity)
            for c in chains:
                for k in range(2):
                    m = 2 * c + k
                    put_r(s, c, k, field[s, 0, m] * factor[s], field[s, 1, m] * factor[s])
            start_right(s, C_CONJ)
            yield
            for c, k, real, imag in planes_right(s):
                put_l(s, c, k, real, imag)
            start_left(s, C_CONJ)
            yield
            sum_r = jnp.zeros((WIN, WIN), jnp.float32)
            sum_i = jnp.zeros((WIN, WIN), jnp.float32)
            for c, k, real, imag in planes_left(s):
                dr, di = d_keep[s, 0, 2 * c + k], d_keep[s, 1, 2 * c + k]
                second_r, second_i = win[s, 1], win[s, 3]
                sum_r = sum_r + (dr * real + di * imag)
                sum_i = sum_i + (dr * imag - di * real)
                put_l(s, c, k, second_r * real + second_i * imag, second_r * imag - second_i * real)
            start_left(s, G_CONJ)
            scatter(1, sum_r)
            scatter(3, sum_i)
            yield
            for c, k, real, imag in planes_left(s):
                put_r(s, c, k, real, imag)
            start_right(s, G_CONJ)
            yield
            sum_r = jnp.zeros((WIN, WIN), jnp.float32)
            sum_i = jnp.zeros((WIN, WIN), jnp.float32)
            for c, k, real, imag in planes_right(s):
                m = 2 * c + k
                pr, pi = probe_ref[0, m], probe_ref[1, m]
                first_r, first_i = win[s, 0], win[s, 2]
                sum_r = sum_r + (pr * real + pi * imag)
                sum_i = sum_i + (pr * imag - pi * real)
                grad_r = first_r * real + first_i * imag
                grad_i = first_r * imag - first_i * real
                probe_grad_ref[0, m] = grad_r if s == 0 else probe_grad_ref[0, m] + grad_r
                probe_grad_ref[1, m] = grad_i if s == 0 else probe_grad_ref[1, m] + grad_i
                if s == scans[-1]:
                    for part in range(2):
                        write(part, m).start()
            scatter(0, sum_r)
            scatter(2, sum_i)

        under_way = [steps(s) for s in scans]
        while under_way:
            under_way = [step for step in under_way if next(step, True) is None]

    pl.run_scoped(
        run, *[pltpu.ACC(c)((ROWS, 2 * WIN), jnp.float32) for _ in scans for c in chains for _ in range(BLOCKS)]
    )

    lane_all = lane_iota(ext_rows)
    east = jnp.zeros((ext_rows, LANES), jnp.float32)
    west = jnp.zeros((ext_rows, LANES), jnp.float32)
    for p in range(PLANES):
        for q in range(2):
            cols = slice(q * LANES, (q + 1) * LANES)
            north_rim_ref[p, :, cols] = grad[p, q, 0:HALO, :]
            center_ref[p, :, cols] = grad[p, q, HALO:last, :]
            south_rim_ref[p, :, cols] = grad[p, q, last:ext_rows, :]
        third = grad[p, 2]
        here = (lane_all >= p * HALO) & (lane_all < (p + 1) * HALO)
        east = jnp.where(here, turned(third, p * HALO), east)
        west = jnp.where(here, turned(third, (p - 3) * HALO), west)
    east_rim_ref[...] = east
    west_rim_ref[...] = west
    for part in range(2):
        for m in range(MODES):
            write(part, m).wait()


def rim_corner_kernel(from_west_ref, from_east_ref, to_north_ref, to_south_ref):
    for k, ref in enumerate((from_west_ref, from_east_ref)):
        to_north_ref[k * HALO : (k + 1) * HALO, :] = ref[0:HALO, :]
        to_south_ref[k * HALO : (k + 1) * HALO, :] = ref[ref.shape[0] - HALO :, :]


def share_kernel(parts_ref, share_ref, block, sem):
    repeats = block.shape[0]
    block[...] = jnp.broadcast_to(jnp.sum(parts_ref[...], axis=0)[None], block.shape)
    copies = [
        pltpu.make_async_copy(block, share_ref.at[k * repeats : (k + 1) * repeats], sem.at[k])
        for k in range(share_ref.shape[0] // repeats)
    ]
    for copy in copies:
        copy.start()
    for copy in copies:
        copy.wait()


def from_sides(left, right, p):
    lane = lane_iota(left.shape[0])
    return (
        jnp.where(lane < HALO, turned(left, -p * HALO), 0.0),
        jnp.where(lane >= LANES - HALO, turned(right, (3 - p) * HALO), 0.0),
    )


def object_kernel(
    center_ref, from_north_ref, from_south_ref, from_west_ref, from_east_ref, object_ref, north_ref, south_ref
):
    rows = center_ref.shape[1]
    for p in range(PLANES):
        sides = from_sides(from_west_ref[HALO : HALO + rows, :], from_east_ref[HALO : HALO + rows, :], p)
        for q in range(2):
            cols = slice(q * LANES, (q + 1) * LANES)
            whole = center_ref[p, :, cols] + sides[q]
            object_ref[p, :, cols] = whole
            north_ref[p, :, cols] = whole[0:HALO] + from_north_ref[p, :, cols]
            south_ref[p, :, cols] = whole[rows - HALO :] + from_south_ref[p, :, cols]


def final_kernel(
    object_in, north_ref, south_ref, north_corners_ref, south_corners_ref, total_ref, probe_ref,
    object_ref, probe_new_ref, strips, steps, sem,
):
    del object_in
    rows = object_ref.shape[1]
    copies = []
    for k, (edge_ref, corners_ref) in enumerate(((north_ref, north_corners_ref), (south_ref, south_corners_ref))):
        for p in range(PLANES):
            corners = from_sides(corners_ref[0:HALO, :], corners_ref[HALO:, :], p)
            for q in range(2):
                cols = slice(q * LANES, (q + 1) * LANES)
                strips[k, p, :, cols] = edge_ref[p, :, cols] + corners[q]
        place_at = slice(0, HALO) if k == 0 else slice(rows - HALO, rows)
        copies.append(pltpu.make_async_copy(strips.at[k], object_ref.at[:, place_at, :], sem.at[k]))
        copies[-1].start()
    total = total_ref[...]
    squares = jnp.sum(total * total, axis=0, keepdims=True)
    mean = jnp.sum(squares, axis=1, keepdims=True) / (total.shape[0] * total.shape[1])
    scale = STEP_SIZE / jnp.sqrt(mean + EPSILON)
    chunk = total.shape[0] // CHUNKS
    for k in range(CHUNKS):
        part = slice(k * chunk, (k + 1) * chunk)
        steps[part, :] = probe_ref[part, :] - total_ref[part, :] * scale
        copies.append(pltpu.make_async_copy(steps.at[part, :], probe_new_ref.at[part, :], sem.at[2 + k]))
        copies[-1].start()
    for copy in copies:
        copy.wait()


def vmem(count):
    return [pl.BlockSpec(memory_space=pltpu.VMEM)] * count


def f32(*shape):
    return jax.ShapeDtypeStruct(shape, jnp.float32)


def moved(block, axis, distance):
    count = lax.axis_size(axis)
    return lax.ppermute(block, axis, [(i, (i + distance) % count) for i in range(count)])


def cost(us):
    return pl.CostEstimate(flops=int(us * 1e9), bytes_accessed=int(us * 3e6), transcendentals=0)


def call(kernel, outs, ins, scratch=(), scalars=0, limit=2, us=0):
    return pl.pallas_call(
        kernel,
        out_shape=outs,
        in_specs=[pl.BlockSpec(memory_space=pltpu.SMEM)] * scalars + vmem(ins),
        out_specs=vmem(len(outs)) if isinstance(outs, list) else vmem(1)[0],
        scratch_shapes=scratch,
        compiler_params=pltpu.CompilerParams(vmem_limit_bytes=limit * 2**20),
        cost_estimate=cost(us) if us else None,
    )


def main_call(scans, rows, cols):
    ext_rows = rows + 2 * HALO
    pair = pltpu.VMEM((scans, MODES // 2, 2 * WIN, 2 * WIN), jnp.bfloat16)
    modes = pltpu.VMEM((scans, 2, MODES, WIN, WIN), jnp.float32)
    outs = [f32(2, MODES, WIN, WIN), f32(PLANES, rows, cols)]
    outs += [f32(PLANES, HALO, cols)] * 2 + [f32(ext_rows, LANES)] * 2 + [f32(PLANES, 3, ext_rows, LANES)]
    run = pl.pallas_call(
        main_kernel,
        out_shape=outs,
        in_specs=[pl.BlockSpec(memory_space=pltpu.SMEM)] + vmem(8),
        out_specs=[pl.BlockSpec(memory_space=pl.ANY)] + vmem(len(outs) - 1),
        scratch_shapes=[
            pair, pair, pair, pair, modes, modes,
            pltpu.VMEM((scans, PLANES, WIN, WIN), jnp.float32),
            pltpu.VMEM((scans, WIN, WIN), jnp.float32),
            pltpu.VMEM((PLANES, 3, ext_rows, LANES), jnp.float32),
            pltpu.VMEM((2, MODES, WIN, WIN), jnp.float32),
            pltpu.SemaphoreType.DMA((2 * MODES,)),
        ],
        input_output_aliases={1: 6},
        compiler_params=pltpu.CompilerParams(vmem_limit_bytes=24 * 2**20),
        cost_estimate=cost(12),
    )
    return lambda *args: run(*args)[:6]


def on_device(object_tiles, probe_modes, offsets, amplitude):
    rows, cols = object_tiles.shape[2:]
    ext_rows = rows + 2 * HALO
    scans = offsets.shape[2]
    tile = object_tiles.reshape(PLANES, rows, cols)
    offset_pairs = jnp.swapaxes(offsets, 2, 3).reshape(2, scans)
    amp = amplitude.reshape(scans, WIN, WIN)
    flat = (2 * MODES * WIN, WIN)
    mats = jnp.asarray(matrices())
    devices = lax.axis_size("row") * lax.axis_size("col")

    anywhere = pl.BlockSpec(memory_space=pl.ANY)
    north = moved(tile[:, rows - HALO :], "row", 1)
    south = moved(tile[:, :HALO], "row", -1)
    east_send, west_send = call(pack_kernel, [f32(rows, LANES)] * 2, 1, us=1)(tile)
    from_west = moved(east_send, "col", 1)
    from_east = moved(west_send, "col", -1)
    east_send, west_send = call(corner_kernel, [f32(2 * HALO, LANES)] * 2, 2, us=1)(north, south)
    west_corners = moved(east_send, "col", 1)
    east_corners = moved(west_send, "col", -1)

    ext = call(assemble_kernel, f32(PLANES, 3, ext_rows, LANES), 3, us=4)(tile, north, south)
    probe_grad, center, north_rim, south_rim, east_rim, west_rim = main_call(scans, rows, cols)(
        offset_pairs, ext, from_west, from_east, west_corners, east_corners, amp, probe_modes, mats
    )

    parts = lax.all_to_all(probe_grad.reshape(devices, -1, LANES), BOTH, 0, 0, tiled=True)
    rim_from_west = moved(east_rim, "col", 1)
    rim_from_east = moved(west_rim, "col", -1)
    from_south = moved(north_rim, "row", -1)
    from_north = moved(south_rim, "row", 1)
    share = pl.pallas_call(
        share_kernel,
        out_shape=f32(*parts.shape),
        in_specs=vmem(1),
        out_specs=anywhere,
        scratch_shapes=[
            pltpu.VMEM((devices // CHUNKS, *parts.shape[1:]), jnp.float32),
            pltpu.SemaphoreType.DMA((CHUNKS,)),
        ],
        compiler_params=pltpu.CompilerParams(vmem_limit_bytes=2 * 2**20),
    )(parts)
    total = lax.all_to_all(share, BOTH, 0, 0, tiled=True)
    to_north, to_south = call(rim_corner_kernel, [f32(2 * HALO, LANES)] * 2, 2, us=20)(rim_from_west, rim_from_east)
    south_corners = moved(to_north, "row", -1)
    north_corners = moved(to_south, "row", 1)
    edge = f32(PLANES, HALO, cols)
    bulk, north_edge, south_edge = call(object_kernel, [f32(PLANES, rows, cols), edge, edge], 5)(
        center, from_north, from_south, rim_from_west, rim_from_east
    )
    object_grad, probe_new = pl.pallas_call(
        final_kernel,
        out_shape=[f32(PLANES, rows, cols), f32(*flat)],
        in_specs=[anywhere] + vmem(6),
        out_specs=[anywhere] * 2,
        scratch_shapes=[
            pltpu.VMEM((2, PLANES, HALO, cols), jnp.float32),
            pltpu.VMEM(flat, jnp.float32),
            pltpu.SemaphoreType.DMA((2 + CHUNKS,)),
        ],
        input_output_aliases={0: 0},
        compiler_params=pltpu.CompilerParams(vmem_limit_bytes=2 * 2**20),
    )(
        bulk, north_edge, south_edge, north_corners, south_corners, total.reshape(flat), probe_modes.reshape(flat)
    )
    return object_grad.reshape(object_tiles.shape), probe_new.reshape(probe_modes.shape)


def solution(mesh):
    placed = (
        P(None, None, "row", "col"),
        P(),
        P("row", "col", None, None),
        P("row", "col", None, None, None),
    )
    return jax.shard_map(
        on_device,
        mesh=mesh,
        in_specs=placed,
        out_specs=(P(None, None, "row", "col"), P()),
        check_vma=False,
    )
```

```python
import math

import jax
import jax.numpy as jnp
import numpy as np
from jax import lax
from jax.experimental import pallas as pl
from jax.experimental.pallas import tpu as pltpu
from jax.sharding import PartitionSpec as P

HALO = 32
WIN = 128
MODES = 4
PLANES = 4
LANES = 128
PROP = 0.002
SHIFT_AMP = 0.5
STEP_SIZE = 0.5
EPSILON = 1e-06
COL = ("pair", "core")
PEERS = ("row", "pair")
SWAP = [(0, 1), (1, 0)]


def matrices():
    k = np.arange(WIN)
    c = np.exp(-2j * np.pi * (np.outer(k, k) % WIN) / WIN) / np.sqrt(WIN)
    f = ((k + WIN // 2) % WIN - WIN // 2).astype(np.float64)
    g = c.conj() @ np.diag(np.exp(-1j * PROP * f * f)) @ c
    stack = []
    for m in (c, c.conj(), g, g.conj()):
        w = np.block([[m.real, m.imag], [-m.imag, m.real]]).astype(np.float32)
        high = w.astype(jnp.bfloat16)
        low = (w - high.astype(np.float32)).astype(jnp.bfloat16)
        stack.append(np.stack([high, low]))
    return np.stack(stack)


C, C_CONJ, G, G_CONJ = range(4)
BLOCKS = 2
ROWS = 2 * WIN // BLOCKS
CHUNKS = 4


def lane_iota(rows):
    return lax.broadcasted_iota(jnp.int32, (rows, LANES), 1)


def edges(src, rows):
    lane = lane_iota(rows)
    east = jnp.zeros((rows, LANES), jnp.float32)
    west = jnp.zeros((rows, LANES), jnp.float32)
    for p in range(PLANES):
        here = (lane >= p * HALO) & (lane < (p + 1) * HALO)
        east = jnp.where(here, turned(src[p, :, LANES : 2 * LANES], (p - 3) * HALO), east)
        west = jnp.where(here, turned(src[p, :, 0:LANES], p * HALO), west)
    return east, west


def turned(block, shift):
    return pltpu.roll(block, shift % LANES, 1) if shift % LANES else block


def pack_kernel(tile_ref, east_ref, west_ref):
    east_ref[...], west_ref[...] = edges(tile_ref, tile_ref.shape[1])


def corner_kernel(north_ref, south_ref, east_ref, west_ref):
    east_ref[0:HALO, :], west_ref[0:HALO, :] = edges(north_ref, HALO)
    east_ref[HALO:, :], west_ref[HALO:, :] = edges(south_ref, HALO)


def split(value):
    high = value.astype(jnp.bfloat16)
    return high, (value - high.astype(jnp.float32)).astype(jnp.bfloat16)


def dot(left, right):
    return jnp.dot(left, right, preferred_element_type=jnp.float32)


def assemble_kernel(tile_ref, north_ref, south_ref, ext):
    rows = tile_ref.shape[1]
    for p in range(PLANES):
        for q in range(2):
            cols = slice(q * LANES, (q + 1) * LANES)
            ext[p, q, 0:HALO, :] = north_ref[p, :, cols]
            ext[p, q, HALO : HALO + rows, :] = tile_ref[p, :, cols]
            ext[p, q, HALO + rows :, :] = south_ref[p, :, cols]


def place(offsets_ref, s, q_count=3):
    start = lax.rem(offsets_ref[1, s] + (q_count * LANES - HALO), q_count * LANES)
    first = lax.div(start, LANES)
    return offsets_ref[0, s], first, lax.rem(first + 1, q_count), lax.rem(start, LANES)


def main_kernel(
    offsets_ref, core_ref, ext_in, from_west_ref, from_east_ref, west_corners_ref, east_corners_ref, amp_ref, probe_ref, mat_ref,
    keep_ref, send_ref, center_ref, north_rim_ref, south_rim_ref, east_rim_ref, west_rim_ref, ext,
    rh, rl, lh, ll, field, d_keep, win, factor, grad, probe_grad_ref,
):
    del ext_in
    ext_rows = ext.shape[2]
    last = ext_rows - HALO

    def beside(left, right, p):
        low = lane_iota(left.shape[0]) < 2 * HALO
        return jnp.where(low, turned(right, -p * HALO), turned(left, (3 - p) * HALO))

    for p in range(PLANES):
        ext[p, 2, 0:HALO, :] = beside(west_corners_ref[0:HALO, :], east_corners_ref[0:HALO, :], p)
        ext[p, 2, HALO:last, :] = beside(from_west_ref[...], from_east_ref[...], p)
        ext[p, 2, last:ext_rows, :] = beside(west_corners_ref[HALO:, :], east_corners_ref[HALO:, :], p)

    lane = lane_iota(WIN)
    chains = range(MODES // 2)
    scans = range(amp_ref.shape[0])

    def put(high, low, at, value):
        high[at], low[at] = split(value)

    def run(*accs):
        def blocks(s, c):
            first = (s * len(chains) + c) * BLOCKS
            return accs[first : first + BLOCKS]

        def multiply(s, c, rhs, lhss, stage):
            pltpu.matmul_push_rhs(rhs, stage, c)
            for lhs in lhss:
                for b, acc in enumerate(blocks(s, c)):
                    pltpu.matmul_acc_lhs(acc, lhs[b * ROWS : (b + 1) * ROWS, :], stage)
                    stage = None

        def start_right(s, which):
            for c in chains:
                multiply(s, c, mat_ref[which, 0], (rh[s, c], rl[s, c]), 0)
                multiply(s, c, mat_ref[which, 1], (rh[s, c],), 1)

        def start_left(s, which):
            high, low = mat_ref[which ^ 1, 0], mat_ref[which ^ 1, 1]
            for c in chains:
                multiply(s, c, lh[s, c], (high, low), 0)
                multiply(s, c, ll[s, c], (high,), 1)

        def planes_right(s):
            for c in chains:
                out = jnp.concatenate([pltpu.matmul_pop(acc) for acc in blocks(s, c)], axis=0)
                for k in range(2):
                    yield c, k, out[k * WIN : (k + 1) * WIN, 0:WIN], out[k * WIN : (k + 1) * WIN, WIN:]

        def planes_left(s):
            for c in chains:
                out = jnp.concatenate([pltpu.matmul_pop(acc) for acc in blocks(s, c)], axis=0)
                for k in range(2):
                    yield c, k, out[0:WIN, k * WIN : (k + 1) * WIN], out[WIN:, k * WIN : (k + 1) * WIN]

        def put_r(s, c, k, real, imag):
            rows = slice(k * WIN, (k + 1) * WIN)
            put(rh, rl, (s, c, rows, slice(0, WIN)), real)
            put(rh, rl, (s, c, rows, slice(WIN, 2 * WIN)), imag)

        def put_l(s, c, k, real, imag):
            cols = slice(k * WIN, (k + 1) * WIN)
            put(lh, ll, (s, c, slice(0, WIN), cols), real)
            put(lh, ll, (s, c, slice(WIN, 2 * WIN), cols), imag)

        def steps(s):
            row, q, q_next, shift = place(offsets_ref, s)
            back = lax.rem(LANES - shift, LANES)

            def scatter(p, value):
                value = pltpu.roll(value, shift, 1)
                grad[p, q, pl.ds(row, WIN), :] += jnp.where(lane >= shift, value, 0.0)
                grad[p, q_next, pl.ds(row, WIN), :] += jnp.where(lane < shift, value, 0.0)

            for p in range(PLANES):
                a = pltpu.roll(ext[p, q, pl.ds(row, WIN), :], back, 1)
                b = pltpu.roll(ext[p, q_next, pl.ds(row, WIN), :], back, 1)
                win[s, p] = jnp.where(lane < LANES - shift, a, b)
            for c in chains:
                for k in range(2):
                    pr, pi = probe_ref[0, 2 * c + k], probe_ref[1, 2 * c + k]
                    put_r(s, c, k, pr * win[s, 0] - pi * win[s, 2], pr * win[s, 2] + pi * win[s, 0])
            start_right(s, G)
            if s == 0:
                grad[...] = jnp.zeros_like(grad)
            yield
            for c, k, real, imag in planes_right(s):
                put_l(s, c, k, real, imag)
            start_left(s, G)
            yield
            for c, k, real, imag in planes_left(s):
                m = 2 * c + k
                d_keep[s, 0, m] = real
                d_keep[s, 1, m] = imag
                second_r, second_i = win[s, 1], win[s, 3]
                put_l(s, c, k, real * second_r - imag * second_i, real * second_i + imag * second_r)
            start_left(s, C)
            yield
            for c, k, real, imag in planes_left(s):
                put_r(s, c, k, real, imag)
            start_right(s, C)
            yield
            intensity = jnp.full((WIN, WIN), SHIFT_AMP, jnp.float32)
            for c, k, real, imag in planes_right(s):
                m = 2 * c + k
                field[s, 0, m] = real
                field[s, 1, m] = imag
                intensity = intensity + (real * real + imag * imag)
            factor[s] = 2.0 - 2.0 * amp_ref[s] / jnp.sqrt(intensity)
            for c in chains:
                for k in range(2):
                    m = 2 * c + k
                    put_r(s, c, k, field[s, 0, m] * factor[s], field[s, 1, m] * factor[s])
            start_right(s, C_CONJ)
            yield
            for c, k, real, imag in planes_right(s):
                put_l(s, c, k, real, imag)
            start_left(s, C_CONJ)
            yield
            sum_r = jnp.zeros((WIN, WIN), jnp.float32)
            sum_i = jnp.zeros((WIN, WIN), jnp.float32)
            for c, k, real, imag in planes_left(s):
                dr, di = d_keep[s, 0, 2 * c + k], d_keep[s, 1, 2 * c + k]
                second_r, second_i = win[s, 1], win[s, 3]
                sum_r = sum_r + (dr * real + di * imag)
                sum_i = sum_i + (dr * imag - di * real)
                put_l(s, c, k, second_r * real + second_i * imag, second_r * imag - second_i * real)
            start_left(s, G_CONJ)
            scatter(1, sum_r)
            scatter(3, sum_i)
            yield
            for c, k, real, imag in planes_left(s):
                put_r(s, c, k, real, imag)
            start_right(s, G_CONJ)
            yield
            sum_r = jnp.zeros((WIN, WIN), jnp.float32)
            sum_i = jnp.zeros((WIN, WIN), jnp.float32)
            for c, k, real, imag in planes_right(s):
                m = 2 * c + k
                pr, pi = probe_ref[0, m], probe_ref[1, m]
                first_r, first_i = win[s, 0], win[s, 2]
                sum_r = sum_r + (pr * real + pi * imag)
                sum_i = sum_i + (pr * imag - pi * real)
                grad_r = first_r * real + first_i * imag
                grad_i = first_r * imag - first_i * real
                probe_grad_ref[0, m] = grad_r if s == 0 else probe_grad_ref[0, m] + grad_r
                probe_grad_ref[1, m] = grad_i if s == 0 else probe_grad_ref[1, m] + grad_i
            scatter(0, sum_r)
            scatter(2, sum_i)

        under_way = [steps(s) for s in scans]
        while under_way:
            under_way = [step for step in under_way if next(step, True) is None]

    pl.run_scoped(
        run, *[pltpu.ACC(c)((ROWS, 2 * WIN), jnp.float32) for _ in scans for c in chains for _ in range(BLOCKS)]
    )

    keep_ref[...] = probe_grad_ref[core_ref[0]]
    send_ref[...] = probe_grad_ref[1 - core_ref[0]]
    lane_all = lane_iota(ext_rows)
    east = jnp.zeros((ext_rows, LANES), jnp.float32)
    west = jnp.zeros((ext_rows, LANES), jnp.float32)
    for p in range(PLANES):
        for q in range(2):
            cols = slice(q * LANES, (q + 1) * LANES)
            north_rim_ref[p, :, cols] = grad[p, q, 0:HALO, :]
            center_ref[p, :, cols] = grad[p, q, HALO:last, :]
            south_rim_ref[p, :, cols] = grad[p, q, last:ext_rows, :]
        third = grad[p, 2]
        here = (lane_all >= p * HALO) & (lane_all < (p + 1) * HALO)
        east = jnp.where(here, turned(third, p * HALO), east)
        west = jnp.where(here, turned(third, (p - 3) * HALO), west)
    east_rim_ref[...] = east
    west_rim_ref[...] = west


def rim_corner_kernel(from_west_ref, from_east_ref, to_north_ref, to_south_ref):
    for k, ref in enumerate((from_west_ref, from_east_ref)):
        to_north_ref[k * HALO : (k + 1) * HALO, :] = ref[0:HALO, :]
        to_south_ref[k * HALO : (k + 1) * HALO, :] = ref[ref.shape[0] - HALO :, :]


def from_sides(left, right, p):
    lane = lane_iota(left.shape[0])
    return (
        jnp.where(lane < HALO, turned(left, -p * HALO), 0.0),
        jnp.where(lane >= LANES - HALO, turned(right, (3 - p) * HALO), 0.0),
    )


def object_kernel(
    center_ref, from_north_ref, from_south_ref, from_west_ref, from_east_ref, object_ref, north_ref, south_ref
):
    rows = center_ref.shape[1]
    for p in range(PLANES):
        sides = from_sides(from_west_ref[HALO : HALO + rows, :], from_east_ref[HALO : HALO + rows, :], p)
        for q in range(2):
            cols = slice(q * LANES, (q + 1) * LANES)
            whole = center_ref[p, :, cols] + sides[q]
            object_ref[p, :, cols] = whole
            north_ref[p, :, cols] = whole[0:HALO] + from_north_ref[p, :, cols]
            south_ref[p, :, cols] = whole[rows - HALO :] + from_south_ref[p, :, cols]


def final_kernel(
    object_in, north_ref, south_ref, north_corners_ref, south_corners_ref, mine_ref, other_ref, probe_ref, core_ref,
    object_ref, probe_new_ref, strips, steps, sem,
):
    del object_in
    rows = object_ref.shape[1]
    copies = []
    for k, (edge_ref, corners_ref) in enumerate(((north_ref, north_corners_ref), (south_ref, south_corners_ref))):
        for p in range(PLANES):
            corners = from_sides(corners_ref[0:HALO, :], corners_ref[HALO:, :], p)
            for q in range(2):
                cols = slice(q * LANES, (q + 1) * LANES)
                strips[k, p, :, cols] = edge_ref[p, :, cols] + corners[q]
        place_at = slice(0, HALO) if k == 0 else slice(rows - HALO, rows)
        copies.append(pltpu.make_async_copy(strips.at[k], object_ref.at[:, place_at, :], sem.at[k]))
        copies[-1].start()
    squares = jnp.sum(mine_ref[...] * mine_ref[...] + other_ref[...] * other_ref[...], axis=0, keepdims=True)
    mean = jnp.sum(squares, axis=1, keepdims=True) / (2 * mine_ref.shape[0] * mine_ref.shape[1])
    scale = STEP_SIZE / jnp.sqrt(mean + EPSILON)
    core = core_ref[0]
    chunk = mine_ref.shape[0] // CHUNKS
    for k in range(CHUNKS):
        part = slice(k * chunk, (k + 1) * chunk)
        steps[core, part, :] = probe_ref[core, part, :] - mine_ref[part, :] * scale
        steps[1 - core, part, :] = probe_ref[1 - core, part, :] - other_ref[part, :] * scale
        copies.append(pltpu.make_async_copy(steps.at[:, part, :], probe_new_ref.at[:, part, :], sem.at[2 + k]))
        copies[-1].start()
    for copy in copies:
        copy.wait()


def vmem(count):
    return [pl.BlockSpec(memory_space=pltpu.VMEM)] * count


def f32(*shape):
    return jax.ShapeDtypeStruct(shape, jnp.float32)


def axis_count(axes):
    return math.prod(lax.axis_size(a) for a in ((axes,) if isinstance(axes, str) else axes))


def moved(block, axis, distance):
    count = axis_count(axis)
    return lax.ppermute(block, axis, [(i, (i + distance) % count) for i in range(count)])


def cost(us):
    return pl.CostEstimate(flops=int(us * 1e9), bytes_accessed=int(us * 3e6), transcendentals=0)


def call(kernel, outs, ins, scratch=(), scalars=0, limit=2, us=0):
    return pl.pallas_call(
        kernel,
        out_shape=outs,
        in_specs=[pl.BlockSpec(memory_space=pltpu.SMEM)] * scalars + vmem(ins),
        out_specs=vmem(len(outs)) if isinstance(outs, list) else vmem(1)[0],
        scratch_shapes=scratch,
        compiler_params=pltpu.CompilerParams(vmem_limit_bytes=limit * 2**20),
        cost_estimate=cost(us) if us else None,
    )


def main_call(scans, rows, cols):
    ext_rows = rows + 2 * HALO
    pair = pltpu.VMEM((scans, MODES // 2, 2 * WIN, 2 * WIN), jnp.bfloat16)
    modes = pltpu.VMEM((scans, 2, MODES, WIN, WIN), jnp.float32)
    outs = [f32(MODES, WIN, WIN), f32(MODES, WIN, WIN), f32(PLANES, rows, cols)]
    outs += [f32(PLANES, HALO, cols)] * 2 + [f32(ext_rows, LANES)] * 2 + [f32(PLANES, 3, ext_rows, LANES)]
    run = pl.pallas_call(
        main_kernel,
        out_shape=outs,
        in_specs=[pl.BlockSpec(memory_space=pltpu.SMEM)] * 2 + vmem(8),
        out_specs=vmem(len(outs)),
        scratch_shapes=[
            pair, pair, pair, pair, modes, modes,
            pltpu.VMEM((scans, PLANES, WIN, WIN), jnp.float32),
            pltpu.VMEM((scans, WIN, WIN), jnp.float32),
            pltpu.VMEM((PLANES, 3, ext_rows, LANES), jnp.float32),
            pltpu.VMEM((2, MODES, WIN, WIN), jnp.float32),
        ],
        input_output_aliases={2: 7},
        compiler_params=pltpu.CompilerParams(vmem_limit_bytes=24 * 2**20),
        cost_estimate=cost(12),
    )
    return lambda *args: run(*args)[:7]


def on_device(object_tiles, probe_modes, offsets, amplitude):
    rows, cols = object_tiles.shape[2:]
    ext_rows = rows + 2 * HALO
    scans = offsets.shape[2]
    tile = object_tiles.reshape(PLANES, rows, cols)
    core = lax.axis_index("core").astype(jnp.int32).reshape(1)
    offset_pairs = jnp.swapaxes(offsets, 2, 3).reshape(2, scans)
    amp = amplitude.reshape(scans, WIN, WIN)
    flat = (2, MODES * WIN, WIN)
    mats = jnp.asarray(matrices())

    north = moved(tile[:, rows - HALO :], "row", 1)
    south = moved(tile[:, :HALO], "row", -1)
    east_send, west_send = call(pack_kernel, [f32(rows, LANES)] * 2, 1, us=1)(tile)
    from_west = moved(east_send, COL, 1)
    from_east = moved(west_send, COL, -1)
    east_send, west_send = call(corner_kernel, [f32(2 * HALO, LANES)] * 2, 2, us=1)(north, south)
    west_corners = moved(east_send, COL, 1)
    east_corners = moved(west_send, COL, -1)

    ext = call(assemble_kernel, f32(PLANES, 3, ext_rows, LANES), 3, us=4)(tile, north, south)
    keep, send, center, north_rim, south_rim, east_rim, west_rim = main_call(scans, rows, cols)(
        offset_pairs, core, ext, from_west, from_east, west_corners, east_corners, amp, probe_modes, mats
    )

    got = lax.ppermute(send, "core", SWAP)
    half_sum = keep + got
    parts = lax.all_to_all(half_sum.reshape(axis_count(PEERS), -1, LANES), PEERS, 0, 0, tiled=True)
    rim_from_west = moved(east_rim, COL, 1)
    rim_from_east = moved(west_rim, COL, -1)
    from_south = moved(north_rim, "row", -1)
    from_north = moved(south_rim, "row", 1)
    share = jnp.broadcast_to(jnp.sum(parts, axis=0)[None], parts.shape)
    mine = lax.all_to_all(share, PEERS, 0, 0, tiled=True).reshape(MODES * WIN, WIN)
    other = lax.ppermute(mine, "core", SWAP)
    to_north, to_south = call(rim_corner_kernel, [f32(2 * HALO, LANES)] * 2, 2, us=80)(rim_from_west, rim_from_east)
    south_corners = moved(to_north, "row", -1)
    north_corners = moved(to_south, "row", 1)
    edge = f32(PLANES, HALO, cols)
    bulk, north_edge, south_edge = call(object_kernel, [f32(PLANES, rows, cols), edge, edge], 5, us=80)(
        center, from_north, from_south, rim_from_west, rim_from_east
    )
    anywhere = pl.BlockSpec(memory_space=pl.ANY)
    object_grad, probe_new = pl.pallas_call(
        final_kernel,
        out_shape=[f32(PLANES, rows, cols), f32(*flat)],
        in_specs=[anywhere] + vmem(7) + [pl.BlockSpec(memory_space=pltpu.SMEM)],
        out_specs=[anywhere] * 2,
        scratch_shapes=[
            pltpu.VMEM((2, PLANES, HALO, cols), jnp.float32),
            pltpu.VMEM(flat, jnp.float32),
            pltpu.SemaphoreType.DMA((2 + CHUNKS,)),
        ],
        input_output_aliases={0: 0},
        compiler_params=pltpu.CompilerParams(vmem_limit_bytes=2 * 2**20),
    )(
        bulk, north_edge, south_edge, north_corners, south_corners, mine, other, probe_modes.reshape(flat), core
    )
    return object_grad.reshape(object_tiles.shape), probe_new.reshape(probe_modes.shape)


def solution(mesh):
    names = ("row",) + COL
    split_mesh = jax.sharding.Mesh(mesh.devices.reshape(mesh.shape["row"], -1, 2), names)
    placed = (
        P(None, None, "row", COL),
        P(),
        P("row", COL, None, None),
        P("row", COL, None, None, None),
    )
    return jax.shard_map(
        on_device,
        mesh=split_mesh,
        in_specs=placed,
        out_specs=(P(None, None, "row", COL), P()),
        check_vma=False,
    )
```
